256 devices in a mesh: gx: 8 (over z_hi, core), gy: 8 (over z_lo, x), gz: 4 (over y).
Axes of the slice: x: 4, y: 4, z: 8 (z_hi: 4, z_lo: 2; z = z_hi * 2 + z_lo), core: 2. Of those that a mesh axis runs over, the one named last changes fastest.
Arguments:
- start_block: bfloat16 [48, 48, 96, 128], P('gx', 'gy', 'gz'), may hold values from -60 to 60
- locked_orbitals: bfloat16 [48, 48, 96, 384], P('gx', 'gy', 'gz'), may hold values from -5 to 5
- cell_h: bfloat16 [8, 8, 16, 343, 343], P('gx', 'gy', 'gz'), may hold values from -1 to 4, as said below
Outputs:
- orbitals: float32 [48, 48, 96, 128], P('gx', 'gy', 'gz')
The draws below stay inside these ranges and needn't reach their ends.
Inputs may be any that keep to these rules, and one draw needn't show every extreme that they name: `cell_h`: every cell matrix is symmetric.
All inputs are finite; a program needn't handle non-finite values.
Results may differ from the reference program's by a relative error of at most 0.0042.
Values may be sent and summed in bfloat16 or wider, within the bound.
No kernel may reach another device: no remote copies, remote signals or barrier semaphores. Data moves between devices by JAX's collectives and lax.ppermute only.
A program may use at most 64 MiB of HBM per device.

```python
import math
import jax
import jax.numpy as jnp
from jax import lax

ORDER = 6
NODE = 343
APPLY = 6
BLOCK = 128
LOCKED = 384
CELLS_X = 8
CELLS_Y = 8
CELLS_Z = 16
NGX = 48
NGY = 48
NGZ = 96
NODES_ALL = 221184


def locked_draw(key):
    values = jax.random.normal(jax.random.fold_in(key, 11), (NGX, NGY, NGZ, LOCKED), jnp.float32)
    return jnp.clip(values, -5.0, 5.0)


def draw_locked_orbitals(key, part):
    return locked_draw(key).astype(jnp.bfloat16)


def draw_start_block(key, part):
    locked = locked_draw(key)
    mixing = jax.random.normal(jax.random.fold_in(key, 12), (LOCKED, BLOCK), jnp.float32) / math.sqrt(LOCKED)
    signal = jnp.dot(locked.reshape(-1, LOCKED), mixing).reshape(NGX, NGY, NGZ, BLOCK)
    noise = jax.random.normal(jax.random.fold_in(key, 13), (NGX, NGY, NGZ, BLOCK), jnp.float32)
    row_scale = jnp.exp(jax.random.uniform(jax.random.fold_in(key, 14), (NGX, NGY, NGZ, 1), jnp.float32, math.log(0.3), math.log(3.0)))
    column_scale = jnp.exp(jax.random.uniform(jax.random.fold_in(key, 15), (BLOCK,), jnp.float32, math.log(0.5), math.log(5.0)))
    values = row_scale * column_scale * (signal + noise) * 0.7071
    return jnp.clip(values, -60.0, 60.0).astype(jnp.bfloat16)


def draw_cell_h(key, part):
    base_key = jax.random.fold_in(key, 21)

    def slab(slab_index):
        slab_key = jax.random.fold_in(base_key, slab_index)
        diagonal = jax.random.uniform(jax.random.fold_in(slab_key, 1), (CELLS_Y, CELLS_Z, NODE), jnp.float32, 1.0, 3.0)
        off_diagonal = jax.random.uniform(jax.random.fold_in(slab_key, 2), (CELLS_Y, CELLS_Z, NODE, NODE), jnp.float32, -1.0, 1.0)
        symmetric = (off_diagonal + jnp.swapaxes(off_diagonal, 2, 3)) * (0.5 / math.sqrt(NODE))
        identity = jnp.eye(NODE, dtype=jnp.float32)
        return (symmetric + diagonal[..., None] * identity).astype(jnp.bfloat16)
    return lax.map(slab, jnp.arange(CELLS_X))


def setup_inputs(seed: int = 0) -> dict:
    keys = jax.random.split(jax.random.key(seed), 4)
    return {
        "start_block": draw_start_block(jax.random.fold_in(keys[3], 71), 0),
        "locked_orbitals": draw_locked_orbitals(jax.random.fold_in(keys[3], 71), 0),
        "cell_h": draw_cell_h(jax.random.fold_in(keys[3], 71), 0),
    }


filter_low = 3.0
filter_high = 40.0
filter_bottom = 0.5

def split_cells(grown, axis_pos, cell_count):
    head_part = lax.slice_in_dim(grown, 0, ORDER * cell_count, axis=axis_pos)
    head_part = head_part.reshape(grown.shape[:axis_pos] + (cell_count, ORDER) + grown.shape[axis_pos + 1:])
    tail_part = lax.slice_in_dim(grown, ORDER, ORDER * cell_count + 1, stride=ORDER, axis=axis_pos)
    tail_part = jnp.expand_dims(tail_part, axis_pos + 1)
    return jnp.concatenate([head_part, tail_part], axis_pos + 1)

def merge_cells(cell_local, axis_pos, cell_count):
    new_shape = cell_local.shape[:axis_pos] + (cell_count * ORDER,) + cell_local.shape[axis_pos + 2:]
    head_part = lax.slice_in_dim(cell_local, 0, ORDER, axis=axis_pos + 1).reshape(new_shape)
    tail_part = lax.slice_in_dim(cell_local, ORDER, ORDER + 1, axis=axis_pos + 1)
    zero_tail = jnp.zeros(cell_local.shape[:axis_pos + 1] + (ORDER - 1,) + cell_local.shape[axis_pos + 2:], cell_local.dtype)
    tail_part = jnp.concatenate([zero_tail, tail_part], axis_pos + 1).reshape(new_shape)
    zero_layer = jnp.zeros(cell_local.shape[:axis_pos] + (1,) + cell_local.shape[axis_pos + 2:], cell_local.dtype)
    return jnp.concatenate([head_part, zero_layer], axis_pos) + jnp.concatenate([zero_layer, tail_part], axis_pos)

def cell_terms(grown, cell_h):
    count_x, count_y, count_z = (cell_h.shape[0], cell_h.shape[1], cell_h.shape[2])
    block_width = grown.shape[3]
    cell_local = split_cells(grown, 0, count_x)
    cell_local = split_cells(cell_local, 2, count_y)
    cell_local = split_cells(cell_local, 4, count_z)
    cell_local = cell_local.transpose(0, 2, 4, 1, 3, 5, 6).reshape(count_x, count_y, count_z, NODE, block_width)
    products = lax.map(lambda operands: jnp.einsum('bcij,bcjv->bciv', operands[0].astype(jnp.float32), operands[1].astype(jnp.float32)), (cell_h, cell_local))
    side = ORDER + 1
    products = products.reshape(count_x, count_y, count_z, side, side, side, block_width).transpose(0, 3, 1, 4, 2, 5, 6)
    products = merge_cells(products, 4, count_z)
    products = merge_cells(products, 2, count_y)
    return merge_cells(products, 0, count_x)

def wrap_extend(values, axis_pos):
    return jnp.concatenate([values, lax.slice_in_dim(values, 0, 1, axis=axis_pos)], axis_pos)

def wrap_fold(values, axis_pos):
    total = values.shape[axis_pos]
    main_part = lax.slice_in_dim(values, 0, total - 1, axis=axis_pos)
    extra = lax.slice_in_dim(values, total - 1, total, axis=axis_pos)
    first_row = lax.slice_in_dim(main_part, 0, 1, axis=axis_pos) + extra
    return jnp.concatenate([first_row, lax.slice_in_dim(main_part, 1, total - 1, axis=axis_pos)], axis_pos)

def apply_operator(values, cell_h):
    grown = values.astype(jnp.bfloat16)
    grown = wrap_extend(wrap_extend(wrap_extend(grown, 0), 1), 2)
    terms = cell_terms(grown, cell_h)
    return wrap_fold(wrap_fold(wrap_fold(terms, 0), 1), 2)

def normalize(gram_matrix, vectors):
    factor = jnp.linalg.cholesky(gram_matrix)
    inverse = jax.scipy.linalg.solve_triangular(factor, jnp.eye(gram_matrix.shape[0], dtype=jnp.float32), lower=True)
    return jnp.dot(vectors.astype(jnp.float32), inverse.T.astype(jnp.float32), precision=lax.Precision.HIGHEST, preferred_element_type=jnp.float32)

def reference(start_block, locked_orbitals, cell_h):
    half_span = (filter_high - filter_low) / 2.0
    center = (filter_high + filter_low) / 2.0
    sigma_first = half_span / (filter_bottom - center)
    previous = start_block.astype(jnp.float32)
    current = sigma_first / half_span * (apply_operator(start_block, cell_h) - center * previous)
    sigma_now = sigma_first
    for repeat in range(APPLY - 1):
        sigma_next = 1.0 / (2.0 / sigma_first - sigma_now)
        following = 2.0 * sigma_next / half_span * (apply_operator(current, cell_h) - center * current) - sigma_now * sigma_next * previous
        previous = current
        current = following
        sigma_now = sigma_next
    block_width = start_block.shape[3]
    filtered = current.astype(jnp.bfloat16).reshape(-1, block_width)
    locked_flat = locked_orbitals.reshape(-1, LOCKED)
    contract = (((0,), (0,)), ((), ()))
    nodes_total = float(NODES_ALL)
    cross = lax.dot_general(locked_flat.astype(jnp.float32), filtered.astype(jnp.float32), contract, preferred_element_type=jnp.float32)
    coefficient = (cross / nodes_total).astype(jnp.bfloat16)
    projected = filtered.astype(jnp.float32) - jnp.dot(locked_flat.astype(jnp.float32), coefficient.astype(jnp.float32), preferred_element_type=jnp.float32)
    gram_matrix = lax.dot_general(projected.astype(jnp.float32), projected.astype(jnp.float32), contract, precision=lax.Precision.HIGHEST, preferred_element_type=jnp.float32) / nodes_total
    result = normalize(gram_matrix, projected)
    return result.reshape(start_block.shape)
```

```python
import jax
import jax.numpy as jnp
from jax import lax
from jax.sharding import PartitionSpec as P

ORDER = 6
NODE = 343
APPLY = 6
LOCKED = 384


filter_low = 3.0
filter_high = 40.0
filter_bottom = 0.5


def padded_2(cells, sides, width):
    for axis, dim in sides:
        count = lax.axis_size(axis)
        head = lax.slice_in_dim(cells, 0, width, axis=dim)
        tail = lax.slice_in_dim(cells, cells.shape[dim] - width, cells.shape[dim], axis=dim)
        cells = jnp.concatenate(
            [
                lax.ppermute(tail, axis, [(i, (i + 1) % count) for i in range(count)]),
                cells,
                lax.ppermute(head, axis, [((i + 1) % count, i) for i in range(count)]),
            ],
            axis=dim,
        )
    return cells


def passed_along(block, axis, distance):
    devices = range(lax.axis_size(axis))
    route = [((i - distance) % len(devices), i) for i in devices]
    return lax.ppermute(block, axis, route)


def mesh_total(rows):
    axes = ("gx", "gy", "gz")
    count = lax.axis_size(axes)
    chunks = rows.reshape(count, rows.shape[0] // count, rows.shape[1])
    mine = lax.all_to_all(chunks, axes, 0, 0).sum(0)
    return lax.all_to_all(jnp.broadcast_to(mine, chunks.shape), axes, 0, 0).reshape(rows.shape)


def split_cells(grown, axis_pos, cell_count):
    head_part = lax.slice_in_dim(grown, 0, ORDER * cell_count, axis=axis_pos)
    head_part = head_part.reshape(
        grown.shape[:axis_pos] + (cell_count, ORDER) + grown.shape[axis_pos + 1 :]
    )
    tail_part = lax.slice_in_dim(grown, ORDER, ORDER * cell_count + 1, stride=ORDER, axis=axis_pos)
    tail_part = jnp.expand_dims(tail_part, axis_pos + 1)
    return jnp.concatenate([head_part, tail_part], axis_pos + 1)


def merge_cells(cell_local, axis_pos, cell_count):
    new_shape = (
        cell_local.shape[:axis_pos] + (cell_count * ORDER,) + cell_local.shape[axis_pos + 2 :]
    )
    head_part = lax.slice_in_dim(cell_local, 0, ORDER, axis=axis_pos + 1).reshape(new_shape)
    tail_part = lax.slice_in_dim(cell_local, ORDER, ORDER + 1, axis=axis_pos + 1)
    zero_tail = jnp.zeros(
        cell_local.shape[: axis_pos + 1] + (ORDER - 1,) + cell_local.shape[axis_pos + 2 :],
        cell_local.dtype,
    )
    tail_part = jnp.concatenate([zero_tail, tail_part], axis_pos + 1).reshape(new_shape)
    zero_layer = jnp.zeros(
        cell_local.shape[:axis_pos] + (1,) + cell_local.shape[axis_pos + 2 :], cell_local.dtype
    )
    return jnp.concatenate([head_part, zero_layer], axis_pos) + jnp.concatenate(
        [zero_layer, tail_part], axis_pos
    )


def cell_terms(grown, cell_h):
    count_x, count_y, count_z = (cell_h.shape[0], cell_h.shape[1], cell_h.shape[2])
    block_width = grown.shape[3]
    cell_local = split_cells(grown, 0, count_x)
    cell_local = split_cells(cell_local, 2, count_y)
    cell_local = split_cells(cell_local, 4, count_z)
    cell_local = cell_local.transpose(0, 2, 4, 1, 3, 5, 6).reshape(
        count_x, count_y, count_z, NODE, block_width
    )
    products = jnp.einsum(
        "abcij,abcjv->abciv", cell_h, cell_local, preferred_element_type=jnp.float32
    )
    side = ORDER + 1
    products = products.reshape(count_x, count_y, count_z, side, side, side, block_width).transpose(
        0, 3, 1, 4, 2, 5, 6
    )
    products = merge_cells(products, 4, count_z)
    products = merge_cells(products, 2, count_y)
    return merge_cells(products, 0, count_x)


def fold_rims(padded, axis_pos):
    total = padded.shape[axis_pos]
    inner = lax.slice_in_dim(padded, 1, total - 1, axis=axis_pos)
    low_rim = lax.slice_in_dim(padded, 0, 1, axis=axis_pos)
    high_rim = lax.slice_in_dim(padded, total - 1, total, axis=axis_pos)
    first_row = lax.slice_in_dim(inner, 0, 1, axis=axis_pos) + low_rim
    last_row = lax.slice_in_dim(inner, total - 3, total - 2, axis=axis_pos) + high_rim
    middle = lax.slice_in_dim(inner, 1, total - 3, axis=axis_pos)
    return jnp.concatenate([first_row, middle, last_row], axis_pos)


def apply_operator(values, cell_h):
    terms = cell_terms(values.astype(jnp.bfloat16), cell_h)
    padded = padded_2(terms, (("gx", 0), ("gy", 1), ("gz", 2)), 1)
    terms = fold_rims(fold_rims(fold_rims(padded, 0), 1), 2)
    return terms


def normalize(gram_matrix, vectors):
    factor = jnp.linalg.cholesky(gram_matrix)
    inverse = jax.scipy.linalg.solve_triangular(
        factor, jnp.eye(gram_matrix.shape[0], dtype=jnp.float32), lower=True
    )
    return jnp.dot(
        vectors, inverse.T, precision=lax.Precision.HIGHEST, preferred_element_type=jnp.float32
    )


def per_device(start_block, locked_orbitals, cell_h):
    devices = lax.axis_size("gx") * lax.axis_size("gy") * lax.axis_size("gz")
    block_width = start_block.shape[3]
    nodes_total = float(
        start_block.shape[0] * start_block.shape[1] * start_block.shape[2] * devices
    )
    rim_first = passed_along(start_block[0:1], "gx", -1)
    grown = jnp.concatenate([start_block, rim_first], 0)
    rim_second = passed_along(grown[:, 0:1], "gy", -1)
    grown = jnp.concatenate([grown, rim_second], 1)
    rim_third = passed_along(grown[:, :, 0:1], "gz", -1)
    grown = jnp.concatenate([grown, rim_third], 2)
    half_span = (filter_high - filter_low) / 2.0
    center = (filter_high + filter_low) / 2.0
    sigma_first = half_span / (filter_bottom - center)
    previous = grown.astype(jnp.float32)
    current = sigma_first / half_span * (apply_operator(grown, cell_h) - center * previous)
    sigma_now = sigma_first
    for repeat in range(APPLY - 1):
        sigma_next = 1.0 / (2.0 / sigma_first - sigma_now)
        following = (
            2.0 * sigma_next / half_span * (apply_operator(current, cell_h) - center * current)
            - sigma_now * sigma_next * previous
        )
        previous = current
        current = following
        sigma_now = sigma_next
    filtered = current[:-1, :-1, :-1].astype(jnp.bfloat16).reshape(-1, block_width)
    locked_flat = locked_orbitals.reshape(-1, LOCKED)
    contract = (((0,), (0,)), ((), ()))
    wide = [filtered] + [locked_flat[:, i : i + 128] for i in range(0, LOCKED, 128)]
    parts = []
    for i in range(4):
        for j in range(i, 4):
            parts.append(
                lax.dot_general(wide[j], wide[i], contract, preferred_element_type=jnp.float32)
            )
    total = mesh_total(jnp.concatenate(parts, 0)).reshape(10, 128, 128)
    self_gram = total[0]
    cross = total[1:4].reshape(LOCKED, block_width)
    locked_gram = jnp.concatenate(
        [
            jnp.concatenate([total[4], total[5].T, total[6].T], 1),
            jnp.concatenate([total[5], total[7], total[8].T], 1),
            jnp.concatenate([total[6], total[8], total[9]], 1),
        ],
        0,
    )
    coefficient = (cross / nodes_total).astype(jnp.bfloat16)
    coef_wide = coefficient.astype(jnp.float32)
    projected = filtered.astype(jnp.float32) - jnp.dot(
        locked_flat, coefficient, preferred_element_type=jnp.float32
    )
    mixed = lax.dot_general(
        cross,
        coef_wide,
        contract,
        precision=lax.Precision.HIGHEST,
        preferred_element_type=jnp.float32,
    )
    weighted = jnp.dot(
        locked_gram, coef_wide, precision=lax.Precision.HIGHEST, preferred_element_type=jnp.float32
    )
    quadratic = lax.dot_general(
        coef_wide,
        weighted,
        contract,
        precision=lax.Precision.HIGHEST,
        preferred_element_type=jnp.float32,
    )
    gram_matrix = (self_gram - mixed - mixed.T + quadratic) / nodes_total
    result = normalize(gram_matrix, projected)
    return result.reshape(start_block.shape)


def solution(mesh):
    placed = (P("gx", "gy", "gz", None), P("gx", "gy", "gz", None), P("gx", "gy", "gz", None, None))
    return jax.shard_map(
        per_device, mesh=mesh, in_specs=placed, out_specs=P("gx", "gy", "gz", None), check_vma=False
    )
```

```python
import functools

import jax
import jax.numpy as jnp
from jax import lax
from jax.experimental import pallas as pl
from jax.experimental.pallas import tpu as pltpu
from jax.sharding import PartitionSpec as P


ORDER = 6
SIDE = 7
NODE = 343
APPLY = 6
LOCKED = 384
WIDTH = 128

PLANE = 56
CELLS = 4
LAYERS = 6 * CELLS + 1
ROWS = 1408
STEP = 6 * PLANE
CELL_OUT = SIDE * PLANE
CELL_IN = CELL_OUT + 8

filter_low = 3.0
filter_high = 40.0
filter_bottom = 0.5
HALF = (filter_high - filter_low) / 2.0
CENTER = (filter_high + filter_low) / 2.0
SIGMA = HALF / (filter_bottom - CENTER)

F32 = jnp.float32
BF16 = jnp.bfloat16
AXES = ("gx", "gy", "gz")
CONTRACT = (((0,), (0,)), ((), ()))
PARAMS = pltpu.CompilerParams(vmem_limit_bytes=16 * 2**20)
VM = pl.BlockSpec(memory_space=pltpu.VMEM)


def call(kernel, outs, n_in, cost=1_000_000, scratch=(), aliases=None):
    return pl.pallas_call(
        kernel,
        out_shape=[jax.ShapeDtypeStruct(s, d) for s, d in outs],
        in_specs=[VM] * n_in,
        out_specs=[VM] * len(outs),
        scratch_shapes=list(scratch),
        input_output_aliases=aliases or {},
        compiler_params=PARAMS,
        cost_estimate=pl.CostEstimate(flops=cost, bytes_accessed=cost, transcendentals=0),
    )


def passed_along(block, axis, distance):
    devices = range(lax.axis_size(axis))
    route = [((i - distance) % len(devices), i) for i in devices]
    return lax.ppermute(block, axis, route)


def both_ways(low_face, high_face, axis):
    return passed_along(high_face, axis, 1), passed_along(low_face, axis, -1)


def order_kernel(h_ref, out_ref):
    row = lax.broadcasted_iota(jnp.int32, (CELL_IN, NODE), 0)
    col = lax.broadcasted_iota(jnp.int32, (CELL_IN, NODE), 1)
    z, rest = row // PLANE, row % PLANE
    x, y = rest // 8, rest % 8
    pick = jnp.where((x * 49 + y * 7 + z == col) & (y < SIDE) & (z < SIDE), 1.0, 0.0).astype(BF16)
    for k in range(CELLS):
        half = jnp.dot(pick[:CELL_OUT], h_ref[k], preferred_element_type=F32).astype(BF16)
        out_ref[k] = lax.dot_general(
            half, pick, (((1,), (1,)), ((), ())), preferred_element_type=F32
        ).astype(BF16)


def build_kernel(start_ref, x_ref, y_ref, z_ref, out_ref):
    out_ref[...] = jnp.zeros_like(out_ref)
    for x in range(SIDE):
        for y in range(SIDE):
            if x < 6 and y < 6:
                line = start_ref[x, y]
            elif y < 6:
                line = x_ref[0, y]
            else:
                line = y_ref[x, 0]
            out_ref[pl.ds(x * 8 + y, LAYERS - 1, stride=PLANE), :] = line.astype(F32)
        top = z_ref[x].astype(F32)
        out_ref[(LAYERS - 1) * PLANE + x * 8 : (LAYERS - 1) * PLANE + x * 8 + SIDE, :] = top


def multiply(field_ref, h_ref, w_ref, low_ref, high_ref, v_ref):
    for k in range(CELLS):
        y = jnp.dot(h_ref[k], v_ref[k * STEP : k * STEP + CELL_IN, :], preferred_element_type=F32)
        if k:
            w_ref[k * STEP : k * STEP + PLANE, :] += y[:PLANE]
        else:
            w_ref[:PLANE, :] = y[:PLANE]
        w_ref[k * STEP + PLANE : k * STEP + CELL_OUT, :] = y[PLANE:]
    w_ref[LAYERS * PLANE :, :] = jnp.zeros((ROWS - LAYERS * PLANE, WIDTH), F32)
    for ref, x in ((low_ref, 0), (high_ref, ORDER)):
        lines = [w_ref[z * PLANE + x * 8 : z * PLANE + x * 8 + 8, :] for z in range(LAYERS)]
        ref[...] = jnp.concatenate(lines + [jnp.zeros((8, WIDTH), F32)], 0).astype(ref.dtype)


def first_kernel(field_ref, h_ref, w_ref, low_ref, high_ref, v_ref):
    v_ref[...] = field_ref[...].astype(BF16)
    multiply(field_ref, h_ref, w_ref, low_ref, high_ref, v_ref)


def recur(scale, shift, w_ref, below_ref, above_ref, now_ref, old_ref, begin, size):
    w = w_ref[begin : begin + size, :]
    if begin == 0:
        w = w + jnp.concatenate(
            [below_ref[...].astype(F32), jnp.zeros((size - PLANE, WIDTH), F32)], 0
        )
    if begin == (LAYERS - 1) * PLANE:
        w = w + jnp.concatenate(
            [above_ref[...].astype(F32), jnp.zeros((size - PLANE, WIDTH), F32)], 0
        )
    out = scale * (w - CENTER * now_ref[begin : begin + size, :])
    if old_ref is not None:
        out = out - shift * old_ref[begin : begin + size, :]
    return out


CHUNKS = [(i * 112, 112) for i in range(12)] + [(1344, 64)]


def step_kernel(scale, shift, has_old, *refs):
    refs = list(refs)
    w_in, below, above, now = refs[:4]
    old = refs[4] if has_old else None
    h_ref, field_ref, w_ref, low_ref, high_ref, v_ref = refs[4 + has_old :]
    for begin, size in CHUNKS:
        out = recur(scale, shift, w_in, below, above, now, old, begin, size)
        field_ref[begin : begin + size, :] = out
        v_ref[begin : begin + size, :] = out.astype(BF16)
    multiply(field_ref, h_ref, w_ref, low_ref, high_ref, v_ref)


def fold_x_kernel(w_in, below_ref, above_ref, w_ref, low_ref, high_ref):
    for z in range(LAYERS):
        for ref, x in ((below_ref, 0), (above_ref, ORDER)):
            rows = slice(z * PLANE + x * 8, z * PLANE + x * 8 + 8)
            w_ref[rows, :] = w_in[rows, :] + ref[z * 8 : z * 8 + 8, :].astype(F32)
    lines = LAYERS * SIDE
    for ref, y in ((low_ref, 0), (high_ref, ORDER)):
        face = w_ref[pl.ds(y, lines, stride=8), :]
        ref[...] = jnp.concatenate([face, jnp.zeros((1, WIDTH), F32)], 0).astype(ref.dtype)


def fold_y_kernel(w_in, below_ref, above_ref, w_ref, low_ref, high_ref):
    lines = LAYERS * SIDE
    for ref, y in ((below_ref, 0), (above_ref, ORDER)):
        rows = pl.ds(y, lines, stride=8)
        w_ref[rows, :] = w_in[rows, :] + ref[...].astype(F32)[:lines]
    low_ref[...] = w_ref[:PLANE, :].astype(low_ref.dtype)
    high_ref[...] = w_ref[(LAYERS - 1) * PLANE : LAYERS * PLANE, :].astype(high_ref.dtype)


def last_kernel(scale, shift, w_in, below, above, now, old, locked_ref, filtered_ref, parts_ref, field):
    for begin, size in CHUNKS:
        field[begin : begin + size, :] = recur(
            scale, shift, w_in, below, above, now, old, begin, size
        )
    depth = LAYERS - 1
    for x in range(ORDER):
        for y in range(ORDER):
            at = (x * ORDER + y) * depth
            line = field[pl.ds(x * 8 + y, depth, stride=PLANE), :]
            filtered_ref[at : at + depth, :] = line.astype(BF16)
    f = filtered_ref[...]
    parts_ref[:128, :128] = lax.dot_general(f, f, CONTRACT, preferred_element_type=F32)
    for i, (r, c) in enumerate(((128, 0), (0, 128), (128, 128))):
        parts_ref[r : r + 128, c : c + 128] = lax.dot_general(
            locked_ref[:, i * 128 : i * 128 + 128], f, CONTRACT, preferred_element_type=F32
        )


def mesh_total(rows):
    mine = lax.all_to_all(rows, AXES, 0, 0, tiled=True).sum(0, keepdims=True)
    return lax.all_to_all(jnp.broadcast_to(mine, rows.shape), AXES, 0, 0, tiled=True)


def normalize(gram_matrix, vectors):
    factor = jnp.linalg.cholesky(gram_matrix)
    inverse = jax.scipy.linalg.solve_triangular(
        factor, jnp.eye(gram_matrix.shape[0], dtype=F32), lower=True
    )
    return jnp.dot(
        vectors, inverse.T, precision=lax.Precision.HIGHEST, preferred_element_type=F32
    )


LINK = BF16


def per_device(start_block, locked_orbitals, cell_h):
    devices = lax.axis_size(AXES)
    nodes_total = float(
        start_block.shape[0] * start_block.shape[1] * start_block.shape[2] * devices
    )
    rim_x = passed_along(start_block[0:1], "gx", -1)
    low_y = jnp.concatenate([start_block[:, 0:1], rim_x[:, 0:1]], 0)
    rim_y = passed_along(low_y, "gy", -1)
    low_z = jnp.concatenate([start_block[:, :, 0], rim_x[:, :, 0]], 0)
    low_z = jnp.concatenate([low_z, rim_y[:, :, 0]], 1)
    rim_z = passed_along(low_z, "gz", -1)
    h = call(order_kernel, [((CELLS, CELL_OUT, CELL_IN), BF16)], 1, cost=4_000_000)(
        cell_h.reshape(CELLS, NODE, NODE)
    )[0]
    field = call(build_kernel, [((ROWS, WIDTH), F32)], 4)(start_block, rim_x, rim_y, rim_z)[0]

    locked_flat = locked_orbitals.reshape(-1, LOCKED)
    wide = [locked_flat[:, i : i + 128] for i in range(0, LOCKED, 128)]
    blocks = [
        lax.dot_general(wide[j], wide[i], CONTRACT, preferred_element_type=F32)
        for i in range(3)
        for j in range(i, 3)
    ]
    locked_parts = jnp.concatenate(
        [jnp.concatenate(blocks[i : i + 2], 0) for i in (0, 2, 4)], 1
    )
    lg = mesh_total(locked_parts)
    g = [lg[r : r + 128, c : c + 128] for c in (0, 128, 256) for r in (0, 128)]
    locked_gram = jnp.concatenate(
        [
            jnp.concatenate([g[0], g[1].T, g[2].T], 1),
            jnp.concatenate([g[1], g[3], g[4].T], 1),
            jnp.concatenate([g[2], g[4], g[5]], 1),
        ],
        0,
    )

    fields = [((ROWS, WIDTH), F32), ((208, WIDTH), LINK), ((208, WIDTH), LINK)]
    scratch = (pltpu.VMEM((ROWS, WIDTH), BF16),)
    w, low, high = call(first_kernel, fields, 2, scratch=scratch)(field, h)
    old, now = None, field
    scale, shift, sigma = SIGMA / HALF, 0.0, SIGMA
    for repeat in range(APPLY):
        below, above = both_ways(low, high, "gx")
        w, low, high = call(
            fold_x_kernel, [((ROWS, WIDTH), F32)] + [((176, WIDTH), LINK)] * 2, 3, aliases={0: 0}
        )(w, below, above)
        below, above = both_ways(low, high, "gy")
        w, low, high = call(
            fold_y_kernel, [((ROWS, WIDTH), F32)] + [((PLANE, WIDTH), LINK)] * 2, 3, aliases={0: 0}
        )(w, below, above)
        below, above = both_ways(low, high, "gz")
        state = (w, below, above, now) + (() if old is None else (old,))
        if repeat < APPLY - 1:
            kernel = functools.partial(step_kernel, scale, shift, old is not None)
            new, w, low, high = call(
                kernel, [((ROWS, WIDTH), F32)] + fields, len(state) + 1, scratch=scratch
            )(*state, h)
            old, now = now, new
            following = 1.0 / (2.0 / SIGMA - sigma)
            scale, shift = 2.0 * following / HALF, sigma * following
            sigma = following
    filtered, parts = call(
        functools.partial(last_kernel, scale, shift),
        [((864, WIDTH), BF16), ((256, 256), F32)],
        6,
        scratch=(pltpu.VMEM((ROWS, WIDTH), F32),),
    )(*state, locked_flat)
    total = mesh_total(parts)
    self_gram = total[:128, :128]
    cross = jnp.concatenate([total[128:, :128], total[:128, 128:], total[128:, 128:]], 0)
    coefficient = (cross / nodes_total).astype(BF16)
    coef_wide = coefficient.astype(F32)
    projected = filtered.astype(F32) - jnp.dot(
        locked_flat, coefficient, preferred_element_type=F32
    )
    precise = dict(precision=lax.Precision.HIGHEST, preferred_element_type=F32)
    mixed = lax.dot_general(cross, coef_wide, CONTRACT, **precise)
    weighted = jnp.dot(locked_gram, coef_wide, **precise)
    quadratic = lax.dot_general(coef_wide, weighted, CONTRACT, **precise)
    gram_matrix = (self_gram - mixed - mixed.T + quadratic) / nodes_total
    result = normalize(gram_matrix, projected)
    return result.reshape(start_block.shape)


def solution(mesh):
    placed = (P("gx", "gy", "gz", None), P("gx", "gy", "gz", None), P("gx", "gy", "gz", None, None))
    return jax.shard_map(
        per_device, mesh=mesh, in_specs=placed, out_specs=P("gx", "gy", "gz", None), check_vma=False
    )
```

```python
import functools

import jax
import jax.numpy as jnp
from jax import lax
from jax.experimental import pallas as pl
from jax.experimental.pallas import tpu as pltpu
from jax.sharding import PartitionSpec as P


ORDER = 6
SIDE = 7
NODE = 343
APPLY = 6
LOCKED = 384
WIDTH = 128

PLANE = 56
CELLS = 4
LAYERS = 6 * CELLS + 1
ROWS = 1408
STEP = 6 * PLANE
CELL_OUT = SIDE * PLANE
CELL_IN = CELL_OUT + 8

filter_low = 3.0
filter_high = 40.0
filter_bottom = 0.5
HALF = (filter_high - filter_low) / 2.0
CENTER = (filter_high + filter_low) / 2.0
SIGMA = HALF / (filter_bottom - CENTER)

F32 = jnp.float32
BF16 = jnp.bfloat16
AXES = ("gx", "gy", "gz")
CONTRACT = (((0,), (0,)), ((), ()))
PARAMS = pltpu.CompilerParams(vmem_limit_bytes=16 * 2**20)
VM = pl.BlockSpec(memory_space=pltpu.VMEM)
SM = pl.BlockSpec(memory_space=pltpu.SMEM)


def call(kernel, outs, n_in, cost=1_000_000, scratch=(), aliases=None, flag=False):
    return pl.pallas_call(
        kernel,
        out_shape=[jax.ShapeDtypeStruct(s, d) for s, d in outs],
        in_specs=[SM] * flag + [VM] * n_in,
        out_specs=[VM] * len(outs),
        scratch_shapes=list(scratch),
        input_output_aliases=aliases or {},
        compiler_params=PARAMS,
        cost_estimate=pl.CostEstimate(flops=cost, bytes_accessed=cost, transcendentals=0),
    )


def passed_along(block, axis, distance):
    devices = range(lax.axis_size(axis))
    route = [((i - distance) % len(devices), i) for i in devices]
    return lax.ppermute(block, axis, route)


def swapped(near, far):
    count = lax.axis_size("gx")
    partner = [(i, i ^ 1) for i in range(count)]
    across = [(i, (i + 2 * (i % 2) - 1) % count) for i in range(count)]
    return lax.ppermute(near, "gx", partner), lax.ppermute(far, "gx", across)


def both_ways(low_face, high_face, axis):
    return passed_along(high_face, axis, 1), passed_along(low_face, axis, -1)


def order_kernel(h_ref, out_ref):
    row = lax.broadcasted_iota(jnp.int32, (CELL_IN, NODE), 0)
    col = lax.broadcasted_iota(jnp.int32, (CELL_IN, NODE), 1)
    z, rest = row // PLANE, row % PLANE
    x, y = rest // 8, rest % 8
    pick = jnp.where((x * 49 + y * 7 + z == col) & (y < SIDE) & (z < SIDE), 1.0, 0.0).astype(BF16)
    for k in range(CELLS):
        half = jnp.dot(pick[:CELL_OUT], h_ref[k], preferred_element_type=F32).astype(BF16)
        out_ref[k] = lax.dot_general(
            half, pick, (((1,), (1,)), ((), ())), preferred_element_type=F32
        ).astype(BF16)


def build_kernel(start_ref, x_ref, y_ref, z_ref, out_ref):
    out_ref[...] = jnp.zeros_like(out_ref)
    for x in range(SIDE):
        for y in range(SIDE):
            if x < 6 and y < 6:
                line = start_ref[x, y]
            elif y < 6:
                line = x_ref[0, y]
            else:
                line = y_ref[x, 0]
            out_ref[pl.ds(x * 8 + y, LAYERS - 1, stride=PLANE), :] = line.astype(F32)
        top = z_ref[x].astype(F32)
        out_ref[(LAYERS - 1) * PLANE + x * 8 : (LAYERS - 1) * PLANE + x * 8 + SIDE, :] = top


def multiply(odd_ref, h_ref, w_ref, near_ref, far_ref, v_ref):
    for k in range(CELLS):
        y = jnp.dot(h_ref[k], v_ref[k * STEP : k * STEP + CELL_IN, :], preferred_element_type=F32)
        if k:
            w_ref[k * STEP : k * STEP + PLANE, :] += y[:PLANE]
        else:
            w_ref[:PLANE, :] = y[:PLANE]
        w_ref[k * STEP + PLANE : k * STEP + CELL_OUT, :] = y[PLANE:]
    w_ref[LAYERS * PLANE :, :] = jnp.zeros((ROWS - LAYERS * PLANE, WIDTH), F32)
    odd = odd_ref[0] == 1
    low, high = (
        jnp.concatenate(
            [w_ref[z * PLANE + x * 8 : z * PLANE + x * 8 + 8, :] for z in range(LAYERS)]
            + [jnp.zeros((8, WIDTH), F32)],
            0,
        )
        for x in (0, ORDER)
    )
    near_ref[...] = jnp.where(odd, low, high).astype(near_ref.dtype)
    far_ref[...] = jnp.where(odd, high, low).astype(far_ref.dtype)


def first_kernel(odd_ref, field_ref, h_ref, w_ref, near_ref, far_ref, v_ref):
    v_ref[...] = field_ref[...].astype(BF16)
    multiply(odd_ref, h_ref, w_ref, near_ref, far_ref, v_ref)


def recur(scale, shift, w_ref, below_ref, above_ref, now_ref, old_ref, begin, size):
    w = w_ref[begin : begin + size, :]
    if begin == 0:
        w = w + jnp.concatenate(
            [below_ref[...].astype(F32), jnp.zeros((size - PLANE, WIDTH), F32)], 0
        )
    if begin == (LAYERS - 1) * PLANE:
        w = w + jnp.concatenate(
            [above_ref[...].astype(F32), jnp.zeros((size - PLANE, WIDTH), F32)], 0
        )
    out = scale * (w - CENTER * now_ref[begin : begin + size, :])
    if old_ref is not None:
        out = out - shift * old_ref[begin : begin + size, :]
    return out


CHUNKS = [(i * 112, 112) for i in range(12)] + [(1344, 64)]


def step_kernel(scale, shift, has_old, odd_ref, *refs):
    refs = list(refs)
    w_in, below, above, now = refs[:4]
    old = refs[4] if has_old else None
    h_ref, field_ref, w_ref, near_ref, far_ref, v_ref = refs[4 + has_old :]
    for begin, size in CHUNKS:
        out = recur(scale, shift, w_in, below, above, now, old, begin, size)
        field_ref[begin : begin + size, :] = out
        v_ref[begin : begin + size, :] = out.astype(BF16)
    multiply(odd_ref, h_ref, w_ref, near_ref, far_ref, v_ref)


def fold_x_kernel(odd_ref, w_in, near_ref, far_ref, w_ref, low_ref, high_ref):
    odd = odd_ref[0] == 1
    for z in range(LAYERS):
        near = near_ref[z * 8 : z * 8 + 8, :].astype(F32)
        far = far_ref[z * 8 : z * 8 + 8, :].astype(F32)
        for x, add in ((0, jnp.where(odd, near, far)), (ORDER, jnp.where(odd, far, near))):
            rows = slice(z * PLANE + x * 8, z * PLANE + x * 8 + 8)
            w_ref[rows, :] = w_in[rows, :] + add
    lines = LAYERS * SIDE
    for ref, y in ((low_ref, 0), (high_ref, ORDER)):
        face = w_ref[pl.ds(y, lines, stride=8), :]
        ref[...] = jnp.concatenate([face, jnp.zeros((1, WIDTH), F32)], 0).astype(ref.dtype)


def fold_y_kernel(w_in, below_ref, above_ref, w_ref, low_ref, high_ref):
    lines = LAYERS * SIDE
    for ref, y in ((below_ref, 0), (above_ref, ORDER)):
        rows = pl.ds(y, lines, stride=8)
        w_ref[rows, :] = w_in[rows, :] + ref[...].astype(F32)[:lines]
    low_ref[...] = w_ref[:PLANE, :].astype(low_ref.dtype)
    high_ref[...] = w_ref[(LAYERS - 1) * PLANE : LAYERS * PLANE, :].astype(high_ref.dtype)


def last_kernel(scale, shift, w_in, below, above, now, old, locked_ref, filtered_ref, parts_ref, field):
    for begin, size in CHUNKS:
        field[begin : begin + size, :] = recur(
            scale, shift, w_in, below, above, now, old, begin, size
        )
    depth = LAYERS - 1
    for x in range(ORDER):
        for y in range(ORDER):
            at = (x * ORDER + y) * depth
            line = field[pl.ds(x * 8 + y, depth, stride=PLANE), :]
            filtered_ref[at : at + depth, :] = line.astype(BF16)
    f = filtered_ref[...]
    parts_ref[:128, :128] = lax.dot_general(f, f, CONTRACT, preferred_element_type=F32)
    for i, (r, c) in enumerate(((128, 0), (0, 128), (128, 128))):
        parts_ref[r : r + 128, c : c + 128] = lax.dot_general(
            locked_ref[:, i * 128 : i * 128 + 128], f, CONTRACT, preferred_element_type=F32
        )


def mesh_total(rows):
    mine = lax.all_to_all(rows, AXES, 0, 0, tiled=True).sum(0, keepdims=True)
    return lax.all_to_all(jnp.broadcast_to(mine, rows.shape), AXES, 0, 0, tiled=True)


PANEL = 16
PIVOTS = 4


def inverse_kernel(a_ref, out_ref, m_ref):
    size = a_ref.shape[0]
    m_ref[:, :size] = a_ref[...]
    r = lax.broadcasted_iota(jnp.int32, (size, size), 0)
    c = lax.broadcasted_iota(jnp.int32, (size, size), 1)
    m_ref[:, size:] = jnp.where(r == c, 1.0, 0.0)
    line = lax.broadcasted_iota(jnp.int32, (PANEL, 2 * size), 0)

    def panel(step, carry):
        p = m_ref[:PANEL, :]
        scale = jnp.ones((PANEL, 2 * size), F32)
        for i in range(0, PANEL, PIVOTS):
            span = range(PIVOTS)
            rows = [jnp.broadcast_to(p[i + u : i + u + 1, :], p.shape) for u in span]
            cols = [jnp.broadcast_to(p[:, i + u : i + u + 1], p.shape) for u in span]
            s = [
                [jnp.broadcast_to(rows[u][:, i + v : i + v + 1], p.shape) for v in span]
                for u in span
            ]
            for u in span:
                inv = 1.0 / s[u][u]
                scale = jnp.where(line == i + u, lax.rsqrt(s[u][u]), scale)
                for v in range(u + 1, PIVOTS):
                    f = s[u][v] * inv
                    rows[v] = rows[v] - f * rows[u]
                    cols[v] = cols[v] - f * cols[u]
                    for w in range(v, PIVOTS):
                        s[v][w] = s[v][w] - f * s[u][w]
                cols[u] = cols[u] * inv
            new = p
            for u in span:
                new = new - cols[u] * rows[u]
            p = jnp.where(line >= i + PIVOTS, new, p)
            for u in span:
                p = jnp.where(line == i + u, rows[u], p)
        p = p * scale
        out_ref[pl.ds(pl.multiple_of(step * PANEL, PANEL), PANEL), :] = p[:, size:]
        update = lax.dot_general(
            p[:, :size], p, CONTRACT, precision=lax.Precision.HIGHEST, preferred_element_type=F32
        )
        left = m_ref[PANEL:, :] - update[PANEL:, :]
        m_ref[: size - PANEL, :size] = pltpu.roll(left[:, :size], size - PANEL, 1)
        m_ref[: size - PANEL, size:] = left[:, size:]
        return carry

    lax.fori_loop(0, size // PANEL, panel, 0)


def normalize(gram_matrix, vectors):
    size = gram_matrix.shape[0]
    inverse = call(
        inverse_kernel, [((size, size), F32)], 1, scratch=(pltpu.VMEM((size, 2 * size), F32),)
    )(gram_matrix)[0]
    return lax.dot_general(
        vectors,
        inverse,
        (((1,), (1,)), ((), ())),
        precision=lax.Precision.HIGHEST,
        preferred_element_type=F32,
    )


LINK = BF16


def per_device(start_block, locked_orbitals, cell_h):
    devices = lax.axis_size(AXES)
    nodes_total = float(
        start_block.shape[0] * start_block.shape[1] * start_block.shape[2] * devices
    )
    rim_x = passed_along(start_block[0:1], "gx", -1)
    low_y = jnp.concatenate([start_block[:, 0:1], rim_x[:, 0:1]], 0)
    rim_y = passed_along(low_y, "gy", -1)
    low_z = jnp.concatenate([start_block[:, :, 0], rim_x[:, :, 0]], 0)
    low_z = jnp.concatenate([low_z, rim_y[:, :, 0]], 1)
    rim_z = passed_along(low_z, "gz", -1)
    h = call(order_kernel, [((CELLS, CELL_OUT, CELL_IN), BF16)], 1, cost=4_000_000)(
        cell_h.reshape(CELLS, NODE, NODE)
    )[0]
    field = call(build_kernel, [((ROWS, WIDTH), F32)], 4)(start_block, rim_x, rim_y, rim_z)[0]

    locked_flat = locked_orbitals.reshape(-1, LOCKED)
    wide = [locked_flat[:, i : i + 128] for i in range(0, LOCKED, 128)]
    blocks = [
        lax.dot_general(wide[j], wide[i], CONTRACT, preferred_element_type=F32)
        for i in range(3)
        for j in range(i, 3)
    ]
    locked_parts = jnp.concatenate(
        [jnp.concatenate(blocks[i : i + 2], 0) for i in (0, 2, 4)], 1
    )

    fields = [((ROWS, WIDTH), F32), ((208, WIDTH), LINK), ((208, WIDTH), LINK)]
    scratch = (pltpu.VMEM((ROWS, WIDTH), BF16),)
    odd = (lax.axis_index("gx") % 2).astype(jnp.int32).reshape(1)
    w, near, far = call(first_kernel, fields, 2, scratch=scratch, flag=True)(odd, field, h)
    old, now = None, field
    scale, shift, sigma = SIGMA / HALF, 0.0, SIGMA
    for repeat in range(APPLY):
        near, far = swapped(near, far)
        w, low, high = call(
            fold_x_kernel,
            [((ROWS, WIDTH), F32)] + [((176, WIDTH), LINK)] * 2,
            3,
            aliases={1: 0},
            flag=True,
        )(odd, w, near, far)
        below, above = both_ways(low, high, "gy")
        w, low, high = call(
            fold_y_kernel, [((ROWS, WIDTH), F32)] + [((PLANE, WIDTH), LINK)] * 2, 3, aliases={0: 0}
        )(w, below, above)
        below, above = both_ways(low, high, "gz")
        state = (w, below, above, now) + (() if old is None else (old,))
        if repeat < APPLY - 1:
            kernel = functools.partial(step_kernel, scale, shift, old is not None)
            new, w, near, far = call(
                kernel, [((ROWS, WIDTH), F32)] + fields, len(state) + 1, scratch=scratch, flag=True
            )(odd, *state, h)
            old, now = now, new
            following = 1.0 / (2.0 / SIGMA - sigma)
            scale, shift = 2.0 * following / HALF, sigma * following
            sigma = following
    filtered, parts = call(
        functools.partial(last_kernel, scale, shift),
        [((864, WIDTH), BF16), ((256, 256), F32)],
        6,
        scratch=(pltpu.VMEM((ROWS, WIDTH), F32),),
    )(*state, locked_flat)
    total = mesh_total(jnp.concatenate([parts, locked_parts], 1))
    g = [total[r : r + 128, c : c + 128] for c in (256, 384, 512) for r in (0, 128)]
    locked_gram = jnp.concatenate(
        [
            jnp.concatenate([g[0], g[1].T, g[2].T], 1),
            jnp.concatenate([g[1], g[3], g[4].T], 1),
            jnp.concatenate([g[2], g[4], g[5]], 1),
        ],
        0,
    )
    self_gram = total[:128, :128]
    cross = jnp.concatenate([total[128:, :128], total[:128, 128:256], total[128:, 128:256]], 0)
    coefficient = (cross / nodes_total).astype(BF16)
    coef_wide = coefficient.astype(F32)
    projected = filtered.astype(F32) - jnp.dot(
        locked_flat, coefficient, preferred_element_type=F32
    )
    precise = dict(precision=lax.Precision.HIGHEST, preferred_element_type=F32)
    mixed = lax.dot_general(cross, coef_wide, CONTRACT, **precise)
    weighted = jnp.dot(locked_gram, coef_wide, **precise)
    quadratic = lax.dot_general(coef_wide, weighted, CONTRACT, **precise)
    gram_matrix = (self_gram - mixed - mixed.T + quadratic) / nodes_total
    result = normalize(gram_matrix, projected)
    return result.reshape(start_block.shape)


def solution(mesh):
    placed = (P("gx", "gy", "gz", None), P("gx", "gy", "gz", None), P("gx", "gy", "gz", None, None))
    return jax.shard_map(
        per_device, mesh=mesh, in_specs=placed, out_specs=P("gx", "gy", "gz", None), check_vma=False
    )
```

```python
import functools

import jax
import jax.numpy as jnp
from jax import lax
from jax.experimental import pallas as pl
from jax.experimental.pallas import tpu as pltpu
from jax.sharding import PartitionSpec as P


ORDER = 6
SIDE = 7
NODE = 343
APPLY = 6
LOCKED = 384
WIDTH = 128

PLANE = 56
CELLS = 4
LAYERS = 6 * CELLS + 1
ROWS = 1408
STEP = 6 * PLANE
CELL_OUT = SIDE * PLANE
CELL_IN = CELL_OUT + 8

filter_low = 3.0
filter_high = 40.0
filter_bottom = 0.5
HALF = (filter_high - filter_low) / 2.0
CENTER = (filter_high + filter_low) / 2.0
SIGMA = HALF / (filter_bottom - CENTER)

F32 = jnp.float32
BF16 = jnp.bfloat16
AXES = ("gx", "gy", "gz")
CONTRACT = (((0,), (0,)), ((), ()))
PARAMS = pltpu.CompilerParams(vmem_limit_bytes=16 * 2**20)
VM = pl.BlockSpec(memory_space=pltpu.VMEM)
SM = pl.BlockSpec(memory_space=pltpu.SMEM)


def call(kernel, outs, n_in, cost=1_000_000, scratch=(), aliases=None, scalars=0):
    return pl.pallas_call(
        kernel,
        out_shape=[jax.ShapeDtypeStruct(s, d) for s, d in outs],
        in_specs=[SM] * scalars + [VM] * n_in,
        out_specs=[VM] * len(outs),
        scratch_shapes=list(scratch),
        input_output_aliases=aliases or {},
        compiler_params=PARAMS,
        cost_estimate=pl.CostEstimate(flops=cost, bytes_accessed=cost, transcendentals=0),
    )


def passed_along(block, axis, distance):
    devices = range(lax.axis_size(axis))
    route = [((i - distance) % len(devices), i) for i in devices]
    return lax.ppermute(block, axis, route)


def swapped(near, far):
    count = lax.axis_size("gx")
    partner = [(i, i ^ 1) for i in range(count)]
    across = [(i, (i + 2 * (i % 2) - 1) % count) for i in range(count)]
    return lax.ppermute(near, "gx", partner), lax.ppermute(far, "gx", across)


def both_ways(low_face, high_face, axis):
    return passed_along(high_face, axis, 1), passed_along(low_face, axis, -1)


def order_kernel(h_ref, out_ref):
    row = lax.broadcasted_iota(jnp.int32, (CELL_IN, NODE), 0)
    col = lax.broadcasted_iota(jnp.int32, (CELL_IN, NODE), 1)
    z, rest = row // PLANE, row % PLANE
    x, y = rest // 8, rest % 8
    pick = jnp.where((x * 49 + y * 7 + z == col) & (y < SIDE) & (z < SIDE), 1.0, 0.0).astype(BF16)
    for k in range(CELLS):
        half = jnp.dot(pick[:CELL_OUT], h_ref[k], preferred_element_type=F32).astype(BF16)
        out_ref[k] = lax.dot_general(
            half, pick, (((1,), (1,)), ((), ())), preferred_element_type=F32
        ).astype(BF16)


def build_kernel(start_ref, x_ref, y_ref, z_ref, out_ref):
    out_ref[...] = jnp.zeros_like(out_ref)
    for x in range(SIDE):
        for y in range(SIDE):
            if x < 6 and y < 6:
                line = start_ref[x, y]
            elif y < 6:
                line = x_ref[0, y]
            else:
                line = y_ref[x, 0]
            out_ref[pl.ds(x * 8 + y, LAYERS - 1, stride=PLANE), :] = line.astype(F32)
        top = z_ref[x].astype(F32)
        out_ref[(LAYERS - 1) * PLANE + x * 8 : (LAYERS - 1) * PLANE + x * 8 + SIDE, :] = top


def multiply(odd_ref, h_ref, w_ref, near_ref, far_ref, v_ref):
    for k in range(CELLS):
        y = jnp.dot(h_ref[k], v_ref[k * STEP : k * STEP + CELL_IN, :], preferred_element_type=F32)
        if k:
            w_ref[k * STEP : k * STEP + PLANE, :] += y[:PLANE]
        else:
            w_ref[:PLANE, :] = y[:PLANE]
        w_ref[k * STEP + PLANE : k * STEP + CELL_OUT, :] = y[PLANE:]
    w_ref[LAYERS * PLANE :, :] = jnp.zeros((ROWS - LAYERS * PLANE, WIDTH), F32)
    odd = odd_ref[0] == 1
    low, high = (
        jnp.concatenate(
            [w_ref[z * PLANE + x * 8 : z * PLANE + x * 8 + 8, :] for z in range(LAYERS)]
            + [jnp.zeros((8, WIDTH), F32)],
            0,
        )
        for x in (0, ORDER)
    )
    near_ref[...] = jnp.where(odd, low, high).astype(near_ref.dtype)
    far_ref[...] = jnp.where(odd, high, low).astype(far_ref.dtype)


def first_kernel(odd_ref, field_ref, h_ref, w_ref, near_ref, far_ref, v_ref):
    v_ref[...] = field_ref[...].astype(BF16)
    multiply(odd_ref, h_ref, w_ref, near_ref, far_ref, v_ref)


def recur(scale, shift, w_ref, below_ref, above_ref, now_ref, old_ref, begin, size):
    w = w_ref[begin : begin + size, :]
    if begin == 0:
        w = w + jnp.concatenate(
            [below_ref[...].astype(F32), jnp.zeros((size - PLANE, WIDTH), F32)], 0
        )
    if begin == (LAYERS - 1) * PLANE:
        w = w + jnp.concatenate(
            [above_ref[...].astype(F32), jnp.zeros((size - PLANE, WIDTH), F32)], 0
        )
    out = scale * (w - CENTER * now_ref[begin : begin + size, :])
    return out - shift * old_ref[begin : begin + size, :]


CHUNKS = [(i * 112, 112) for i in range(12)] + [(1344, 64)]


def step_kernel(
    odd_ref, index_ref, factor_ref, w_in, below, above, now, old, h_ref, field_ref, w_ref, near_ref, far_ref, v_ref
):
    at = index_ref[0] * 2
    scale, shift = factor_ref[at], factor_ref[at + 1]
    for begin, size in CHUNKS:
        out = recur(scale, shift, w_in, below, above, now, old, begin, size)
        field_ref[begin : begin + size, :] = out
        v_ref[begin : begin + size, :] = out.astype(BF16)
    multiply(odd_ref, h_ref, w_ref, near_ref, far_ref, v_ref)


def fold_x_kernel(odd_ref, w_in, near_ref, far_ref, w_ref, low_ref, high_ref):
    odd = odd_ref[0] == 1
    for z in range(LAYERS):
        near = near_ref[z * 8 : z * 8 + 8, :].astype(F32)
        far = far_ref[z * 8 : z * 8 + 8, :].astype(F32)
        for x, add in ((0, jnp.where(odd, near, far)), (ORDER, jnp.where(odd, far, near))):
            rows = slice(z * PLANE + x * 8, z * PLANE + x * 8 + 8)
            w_ref[rows, :] = w_in[rows, :] + add
    lines = LAYERS * SIDE
    for ref, y in ((low_ref, 0), (high_ref, ORDER)):
        face = w_ref[pl.ds(y, lines, stride=8), :]
        ref[...] = jnp.concatenate([face, jnp.zeros((1, WIDTH), F32)], 0).astype(ref.dtype)


def fold_y_kernel(w_in, below_ref, above_ref, w_ref, low_ref, high_ref):
    lines = LAYERS * SIDE
    for ref, y in ((below_ref, 0), (above_ref, ORDER)):
        rows = pl.ds(y, lines, stride=8)
        w_ref[rows, :] = w_in[rows, :] + ref[...].astype(F32)[:lines]
    low_ref[...] = w_ref[:PLANE, :].astype(low_ref.dtype)
    high_ref[...] = w_ref[(LAYERS - 1) * PLANE : LAYERS * PLANE, :].astype(high_ref.dtype)


def last_kernel(scale, shift, w_in, below, above, now, old, locked_ref, filtered_ref, parts_ref, field):
    for begin, size in CHUNKS:
        field[begin : begin + size, :] = recur(
            scale, shift, w_in, below, above, now, old, begin, size
        )
    depth = LAYERS - 1
    for x in range(ORDER):
        for y in range(ORDER):
            at = (x * ORDER + y) * depth
            line = field[pl.ds(x * 8 + y, depth, stride=PLANE), :]
            filtered_ref[at : at + depth, :] = line.astype(BF16)
    f = filtered_ref[...]
    parts_ref[:128, :128] = lax.dot_general(f, f, CONTRACT, preferred_element_type=F32)
    for i, (r, c) in enumerate(((128, 0), (0, 128), (128, 128))):
        parts_ref[r : r + 128, c : c + 128] = lax.dot_general(
            locked_ref[:, i * 128 : i * 128 + 128], f, CONTRACT, preferred_element_type=F32
        )


def mesh_total(rows):
    odd = lax.axis_index("gx") % 2 == 1
    count = lax.axis_size("gx")
    partner = [(i, i ^ 1) for i in range(count)]
    lower, upper = jnp.split(rows, 2)
    other = lax.ppermute(jnp.where(odd, lower, upper), "gx", partner)
    half = jnp.where(odd, upper, lower) + other
    axes = ("gy", "gz")
    pieces = half.reshape(lax.axis_size(axes), -1, rows.shape[1])
    mine = lax.all_to_all(pieces, axes, 0, 0).sum(0)
    total = mine
    for step in range(2, count, 2):
        total = total + passed_along(mine, "gx", step)
    half = lax.all_to_all(jnp.broadcast_to(total, pieces.shape), axes, 0, 0).reshape(half.shape)
    other = lax.ppermute(half, "gx", partner)
    return jnp.concatenate([jnp.where(odd, other, half), jnp.where(odd, half, other)], 0)


PANEL = 16
PIVOTS = 8


def inverse_kernel(a_ref, out_ref, m_ref):
    size = a_ref.shape[0]
    m_ref[:, :size] = a_ref[...]
    r = lax.broadcasted_iota(jnp.int32, (size, size), 0)
    c = lax.broadcasted_iota(jnp.int32, (size, size), 1)
    m_ref[:, size:] = jnp.where(r == c, 1.0, 0.0)
    line = lax.broadcasted_iota(jnp.int32, (PANEL, 2 * size), 0)

    def panel(step, carry):
        p = m_ref[:PANEL, :]
        scale = jnp.ones((PANEL, 2 * size), F32)
        for i in range(0, PANEL, PIVOTS):
            span = range(PIVOTS)
            rows = [jnp.broadcast_to(p[i + u : i + u + 1, :], p.shape) for u in span]
            cols = [jnp.broadcast_to(p[:, i + u : i + u + 1], p.shape) for u in span]
            s = [
                [jnp.broadcast_to(rows[u][:, i + v : i + v + 1], p.shape) for v in span]
                for u in span
            ]
            for u in span:
                inv = 1.0 / s[u][u]
                scale = jnp.where(line == i + u, lax.rsqrt(s[u][u]), scale)
                for v in range(u + 1, PIVOTS):
                    f = s[u][v] * inv
                    rows[v] = rows[v] - f * rows[u]
                    cols[v] = cols[v] - f * cols[u]
                    for w in range(v, PIVOTS):
                        s[v][w] = s[v][w] - f * s[u][w]
                cols[u] = cols[u] * inv
            new = p
            for u in span:
                new = new - cols[u] * rows[u]
            p = jnp.where(line >= i + PIVOTS, new, p)
            for u in span:
                p = jnp.where(line == i + u, rows[u], p)
        p = p * scale
        out_ref[pl.ds(pl.multiple_of(step * PANEL, PANEL), PANEL), :] = p[:, size:]
        update = lax.dot_general(
            p[:, :size], p, CONTRACT, precision=lax.Precision.HIGHEST, preferred_element_type=F32
        )
        left = m_ref[PANEL:, :] - update[PANEL:, :]
        m_ref[: size - PANEL, :size] = pltpu.roll(left[:, :size], size - PANEL, 1)
        m_ref[: size - PANEL, size:] = left[:, size:]
        return carry

    lax.fori_loop(0, size // PANEL, panel, 0)


def normalize(gram_matrix, vectors):
    size = gram_matrix.shape[0]
    inverse = call(
        inverse_kernel, [((size, size), F32)], 1, scratch=(pltpu.VMEM((size, 2 * size), F32),)
    )(gram_matrix)[0]
    return lax.dot_general(
        vectors,
        inverse,
        (((1,), (1,)), ((), ())),
        precision=lax.Precision.HIGHEST,
        preferred_element_type=F32,
    )


LINK = BF16


def per_device(start_block, locked_orbitals, cell_h):
    devices = lax.axis_size(AXES)
    nodes_total = float(
        start_block.shape[0] * start_block.shape[1] * start_block.shape[2] * devices
    )
    rim_x = passed_along(start_block[0:1], "gx", -1)
    low_y = jnp.concatenate([start_block[:, 0:1], rim_x[:, 0:1]], 0)
    rim_y = passed_along(low_y, "gy", -1)
    low_z = jnp.concatenate([start_block[:, :, 0], rim_x[:, :, 0]], 0)
    low_z = jnp.concatenate([low_z, rim_y[:, :, 0]], 1)
    rim_z = passed_along(low_z, "gz", -1)
    h = call(order_kernel, [((CELLS, CELL_OUT, CELL_IN), BF16)], 1, cost=4_000_000)(
        cell_h.reshape(CELLS, NODE, NODE)
    )[0]
    h = pltpu.with_memory_space_constraint(h, pltpu.VMEM)
    field = call(build_kernel, [((ROWS, WIDTH), F32)], 4)(start_block, rim_x, rim_y, rim_z)[0]

    field = pltpu.with_memory_space_constraint(field, pltpu.VMEM)
    locked_flat = locked_orbitals.reshape(-1, LOCKED)
    wide = [locked_flat[:, i : i + 128] for i in range(0, LOCKED, 128)]
    blocks = [
        lax.dot_general(wide[j], wide[i], CONTRACT, preferred_element_type=F32)
        for i in range(3)
        for j in range(i, 3)
    ]
    locked_parts = jnp.concatenate(
        [jnp.concatenate(blocks[i : i + 2], 0) for i in (0, 2, 4)], 1
    )

    fields = [((ROWS, WIDTH), F32), ((208, WIDTH), LINK), ((208, WIDTH), LINK)]
    scratch = (pltpu.VMEM((ROWS, WIDTH), BF16),)
    odd = (lax.axis_index("gx") % 2).astype(jnp.int32).reshape(1)
    w, near, far = call(first_kernel, fields, 2, scratch=scratch, scalars=1)(odd, field, h)
    w = pltpu.with_memory_space_constraint(w, pltpu.VMEM)
    factors, sigma = [(SIGMA / HALF, 0.0)], SIGMA
    for repeat in range(APPLY - 1):
        following = 1.0 / (2.0 / SIGMA - sigma)
        factors.append((2.0 * following / HALF, sigma * following))
        sigma = following
    table = jnp.array(factors[:-1], F32).reshape(-1)

    def exchange(w, near, far):
        near, far = swapped(near, far)
        w, low, high = call(
            fold_x_kernel,
            [((ROWS, WIDTH), F32)] + [((176, WIDTH), LINK)] * 2,
            3,
            aliases={1: 0},
            scalars=1,
        )(odd, w, near, far)
        below, above = both_ways(low, high, "gy")
        w, low, high = call(
            fold_y_kernel, [((ROWS, WIDTH), F32)] + [((PLANE, WIDTH), LINK)] * 2, 3, aliases={0: 0}
        )(w, below, above)
        below, above = both_ways(low, high, "gz")
        return w, below, above

    def apply(repeat, carry, aliases):
        w, near, far, now, old = carry
        w, below, above = exchange(w, near, far)
        index = jnp.asarray(repeat, jnp.int32).reshape(1)
        new, w, near, far = call(
            step_kernel,
            [((ROWS, WIDTH), F32)] + fields,
            6,
            scratch=scratch,
            scalars=3,
            aliases=aliases,
        )(odd, index, table, w, below, above, now, old, h)
        new, w = (pltpu.with_memory_space_constraint(a, pltpu.VMEM) for a in (new, w))
        return w, near, far, new, now

    def pair(step, carry):
        for repeat in (2 * step + 1, 2 * step + 2):
            carry = apply(repeat, carry, {3: 1, 7: 0})
        return carry

    carry = apply(0, (w, near, far, field, field), {3: 1})
    w, near, far, now, old = lax.fori_loop(0, (APPLY - 2) // 2, pair, carry)
    state = exchange(w, near, far) + (now, old)
    scale, shift = factors[-1]
    filtered, parts = call(
        functools.partial(last_kernel, scale, shift),
        [((864, WIDTH), BF16), ((256, 256), F32)],
        6,
        scratch=(pltpu.VMEM((ROWS, WIDTH), F32),),
    )(*state, locked_flat)
    total = mesh_total(jnp.concatenate([parts, locked_parts], 1))
    g = [total[r : r + 128, c : c + 128] for c in (256, 384, 512) for r in (0, 128)]
    locked_gram = jnp.concatenate(
        [
            jnp.concatenate([g[0], g[1].T, g[2].T], 1),
            jnp.concatenate([g[1], g[3], g[4].T], 1),
            jnp.concatenate([g[2], g[4], g[5]], 1),
        ],
        0,
    )
    self_gram = total[:128, :128]
    cross = jnp.concatenate([total[128:, :128], total[:128, 128:256], total[128:, 128:256]], 0)
    coefficient = (cross / nodes_total).astype(BF16)
    coef_wide = coefficient.astype(F32)
    projected = filtered.astype(F32) - jnp.dot(
        locked_flat, coefficient, preferred_element_type=F32
    )
    precise = dict(precision=lax.Precision.HIGHEST, preferred_element_type=F32)
    mixed = lax.dot_general(cross, coef_wide, CONTRACT, **precise)
    weighted = jnp.dot(locked_gram, coef_wide, **precise)
    quadratic = lax.dot_general(coef_wide, weighted, CONTRACT, **precise)
    gram_matrix = (self_gram - mixed - mixed.T + quadratic) / nodes_total
    result = normalize(gram_matrix, projected)
    return result.reshape(start_block.shape)


def solution(mesh):
    placed = (P("gx", "gy", "gz", None), P("gx", "gy", "gz", None), P("gx", "gy", "gz", None, None))
    return jax.shard_map(
        per_device, mesh=mesh, in_specs=placed, out_specs=P("gx", "gy", "gz", None), check_vma=False
    )
```

```python
import functools

import jax
import jax.numpy as jnp
from jax import lax
from jax.experimental import pallas as pl
from jax.experimental.pallas import tpu as pltpu
from jax.sharding import PartitionSpec as P


ORDER = 6
SIDE = 7
NODE = 343
APPLY = 6
LOCKED = 384
WIDTH = 128

PLANE = 56
CELLS = 4
LAYERS = 6 * CELLS + 1
ROWS = 1408
STEP = 6 * PLANE
CELL_OUT = SIDE * PLANE
CELL_IN = CELL_OUT + 8

filter_low = 3.0
filter_high = 40.0
filter_bottom = 0.5
HALF = (filter_high - filter_low) / 2.0
CENTER = (filter_high + filter_low) / 2.0
SIGMA = HALF / (filter_bottom - CENTER)

F32 = jnp.float32
BF16 = jnp.bfloat16
AXES = ("gx", "gy", "gz")
CONTRACT = (((0,), (0,)), ((), ()))
PARAMS = pltpu.CompilerParams(vmem_limit_bytes=16 * 2**20)
VM = pl.BlockSpec(memory_space=pltpu.VMEM)
SM = pl.BlockSpec(memory_space=pltpu.SMEM)


def call(kernel, outs, n_in, cost=1_000_000, scratch=(), aliases=None, scalars=0):
    return pl.pallas_call(
        kernel,
        out_shape=[jax.ShapeDtypeStruct(s, d) for s, d in outs],
        in_specs=[SM] * scalars + [VM] * n_in,
        out_specs=[VM] * len(outs),
        scratch_shapes=list(scratch),
        input_output_aliases=aliases or {},
        compiler_params=PARAMS,
        cost_estimate=pl.CostEstimate(flops=cost, bytes_accessed=cost, transcendentals=0),
    )


def passed_along(block, axis, distance):
    devices = range(lax.axis_size(axis))
    route = [((i - distance) % len(devices), i) for i in devices]
    return lax.ppermute(block, axis, route)


def swapped(near, far):
    count = lax.axis_size("gx")
    partner = [(i, i ^ 1) for i in range(count)]
    across = [(i, (i + 2 * (i % 2) - 1) % count) for i in range(count)]
    return lax.ppermute(near, "gx", partner), lax.ppermute(far, "gx", across)


def both_ways(low_face, high_face, axis):
    return passed_along(high_face, axis, 1), passed_along(low_face, axis, -1)


def order_kernel(h_ref, out_ref):
    row = lax.broadcasted_iota(jnp.int32, (CELL_IN, NODE), 0)
    col = lax.broadcasted_iota(jnp.int32, (CELL_IN, NODE), 1)
    z, rest = row // PLANE, row % PLANE
    x, y = rest // 8, rest % 8
    pick = jnp.where((x * 49 + y * 7 + z == col) & (y < SIDE) & (z < SIDE), 1.0, 0.0).astype(BF16)
    for k in range(CELLS):
        half = jnp.dot(pick[:CELL_OUT], h_ref[k], preferred_element_type=F32).astype(BF16)
        out_ref[k] = lax.dot_general(
            half, pick, (((1,), (1,)), ((), ())), preferred_element_type=F32
        ).astype(BF16)


def multiply(odd_ref, h_ref, w_ref, near_ref, far_ref, v_ref):
    for k in range(CELLS):
        y = jnp.dot(h_ref[k], v_ref[k * STEP : k * STEP + CELL_IN, :], preferred_element_type=F32)
        if k:
            w_ref[k * STEP : k * STEP + PLANE, :] += y[:PLANE]
        else:
            w_ref[:PLANE, :] = y[:PLANE]
        w_ref[k * STEP + PLANE : k * STEP + CELL_OUT, :] = y[PLANE:]
    w_ref[LAYERS * PLANE : ROWS, :] = jnp.zeros((ROWS - LAYERS * PLANE, WIDTH), F32)
    odd = odd_ref[0] == 1
    low, high = (
        jnp.concatenate(
            [w_ref[z * PLANE + x * 8 : z * PLANE + x * 8 + 8, :] for z in range(LAYERS)]
            + [jnp.zeros((8, WIDTH), F32)],
            0,
        )
        for x in (0, ORDER)
    )
    near_ref[...] = jnp.where(odd, low, high).astype(near_ref.dtype)
    far_ref[...] = jnp.where(odd, high, low).astype(far_ref.dtype)


def box(number):
    return pl.multiple_of((1 + number % 2) * ROWS, ROWS)


def first_kernel(odd_ref, start_ref, x_ref, y_ref, z_ref, h_ref, s_ref, near_ref, far_ref, v_ref):
    s_ref[ROWS:, :] = jnp.zeros((2 * ROWS, WIDTH), F32)
    for x in range(SIDE):
        for y in range(SIDE):
            if x < 6 and y < 6:
                line = start_ref[x, y]
            elif y < 6:
                line = x_ref[0, y]
            else:
                line = y_ref[x, 0]
            s_ref[pl.ds(ROWS + x * 8 + y, LAYERS - 1, stride=PLANE), :] = line.astype(F32)
        top = ROWS + (LAYERS - 1) * PLANE + x * 8
        s_ref[top : top + SIDE, :] = z_ref[x].astype(F32)
    for begin, size in CHUNKS:
        v_ref[begin : begin + size, :] = s_ref[ROWS + begin : ROWS + begin + size, :].astype(BF16)
    multiply(odd_ref, h_ref, s_ref, near_ref, far_ref, v_ref)


CHUNKS = [(i * 112, 112) for i in range(12)] + [(1344, 64)]


def recur(scale, shift, s_ref, below_ref, above_ref, now, old, begin, size):
    w = s_ref[begin : begin + size, :]
    for at, face_ref in ((0, below_ref), (CHUNKS[-1][0], above_ref)):
        if begin == at:
            rest = jnp.zeros((size - PLANE, WIDTH), F32)
            w = w + jnp.concatenate([face_ref[...].astype(F32), rest], 0)
    out = scale * (w - CENTER * s_ref[pl.ds(now + begin, size), :])
    return out - shift * s_ref[pl.ds(old + begin, size), :]


def step_kernel(
    odd_ref, index_ref, factor_ref, s_in, below, above, h_ref, s_ref, near_ref, far_ref, v_ref
):
    number = index_ref[0]
    scale, shift = factor_ref[2 * number], factor_ref[2 * number + 1]
    now, old = box(number), box(number + 1)
    for begin, size in CHUNKS:
        out = recur(scale, shift, s_ref, below, above, now, old, begin, size)
        s_ref[pl.ds(old + begin, size), :] = out
        v_ref[begin : begin + size, :] = out.astype(BF16)
    multiply(odd_ref, h_ref, s_ref, near_ref, far_ref, v_ref)


def fold_x_kernel(odd_ref, w_in, near_ref, far_ref, w_ref, low_ref, high_ref):
    odd = odd_ref[0] == 1
    for z in range(LAYERS):
        near = near_ref[z * 8 : z * 8 + 8, :].astype(F32)
        far = far_ref[z * 8 : z * 8 + 8, :].astype(F32)
        for x, add in ((0, jnp.where(odd, near, far)), (ORDER, jnp.where(odd, far, near))):
            rows = slice(z * PLANE + x * 8, z * PLANE + x * 8 + 8)
            w_ref[rows, :] += add
    lines = LAYERS * SIDE
    for ref, y in ((low_ref, 0), (high_ref, ORDER)):
        face = w_ref[pl.ds(y, lines, stride=8), :]
        ref[...] = jnp.concatenate([face, jnp.zeros((1, WIDTH), F32)], 0).astype(ref.dtype)


def fold_y_kernel(w_in, below_ref, above_ref, w_ref, low_ref, high_ref):
    lines = LAYERS * SIDE
    for ref, y in ((below_ref, 0), (above_ref, ORDER)):
        rows = pl.ds(y, lines, stride=8)
        w_ref[rows, :] = w_ref[rows, :] + ref[...].astype(F32)[:lines]
    low_ref[...] = w_ref[:PLANE, :].astype(low_ref.dtype)
    high_ref[...] = w_ref[(LAYERS - 1) * PLANE : LAYERS * PLANE, :].astype(high_ref.dtype)


def last_kernel(scale, shift, s_ref, below, above, locked_ref, filtered_ref, parts_ref, field):
    now, old = (ROWS * (1 + (number % 2)) for number in (APPLY - 1, APPLY))
    for begin, size in CHUNKS:
        field[begin : begin + size, :] = recur(
            scale, shift, s_ref, below, above, now, old, begin, size
        )
    depth = LAYERS - 1
    for x in range(ORDER):
        for y in range(ORDER):
            at = (x * ORDER + y) * depth
            line = field[pl.ds(x * 8 + y, depth, stride=PLANE), :]
            filtered_ref[at : at + depth, :] = line.astype(BF16)
    f = filtered_ref[...]
    parts_ref[:128, :128] = lax.dot_general(f, f, CONTRACT, preferred_element_type=F32)
    for i, (r, c) in enumerate(((128, 0), (0, 128), (128, 128))):
        parts_ref[r : r + 128, c : c + 128] = lax.dot_general(
            locked_ref[:, i * 128 : i * 128 + 128], f, CONTRACT, preferred_element_type=F32
        )


def mesh_total(rows):
    odd = lax.axis_index("gx") % 2 == 1
    count = lax.axis_size("gx")
    partner = [(i, i ^ 1) for i in range(count)]
    lower, upper = jnp.split(rows, 2)
    other = lax.ppermute(jnp.where(odd, lower, upper), "gx", partner)
    half = jnp.where(odd, upper, lower) + other
    axes = ("gy", "gz")
    pieces = half.reshape(lax.axis_size(axes), -1, rows.shape[1])
    mine = lax.all_to_all(pieces, axes, 0, 0).sum(0)
    total = mine
    for step in range(2, count, 2):
        total = total + passed_along(mine, "gx", step)
    half = lax.all_to_all(jnp.broadcast_to(total, pieces.shape), axes, 0, 0).reshape(half.shape)
    other = lax.ppermute(half, "gx", partner)
    return jnp.concatenate([jnp.where(odd, other, half), jnp.where(odd, half, other)], 0)


PANEL = 16
PIVOTS = 8


def inverse_kernel(a_ref, out_ref, m_ref):
    size = a_ref.shape[0]
    m_ref[:, :size] = a_ref[...]
    r = lax.broadcasted_iota(jnp.int32, (size, size), 0)
    c = lax.broadcasted_iota(jnp.int32, (size, size), 1)
    m_ref[:, size:] = jnp.where(r == c, 1.0, 0.0)
    line = lax.broadcasted_iota(jnp.int32, (PANEL, 2 * size), 0)

    def panel(step, carry):
        p = m_ref[:PANEL, :]
        scale = jnp.ones((PANEL, 2 * size), F32)
        for i in range(0, PANEL, PIVOTS):
            span = range(PIVOTS)
            rows = [jnp.broadcast_to(p[i + u : i + u + 1, :], p.shape) for u in span]
            cols = [jnp.broadcast_to(p[:, i + u : i + u + 1], p.shape) for u in span]
            s = [
                [jnp.broadcast_to(rows[u][:, i + v : i + v + 1], p.shape) for v in span]
                for u in span
            ]
            for u in span:
                inv = 1.0 / s[u][u]
                scale = jnp.where(line == i + u, lax.rsqrt(s[u][u]), scale)
                for v in range(u + 1, PIVOTS):
                    f = s[u][v] * inv
                    rows[v] = rows[v] - f * rows[u]
                    cols[v] = cols[v] - f * cols[u]
                    for w in range(v, PIVOTS):
                        s[v][w] = s[v][w] - f * s[u][w]
                cols[u] = cols[u] * inv
            new = p
            for u in span:
                new = new - cols[u] * rows[u]
            p = jnp.where(line >= i + PIVOTS, new, p)
            for u in span:
                p = jnp.where(line == i + u, rows[u], p)
        p = p * scale
        out_ref[pl.ds(pl.multiple_of(step * PANEL, PANEL), PANEL), :] = p[:, size:]
        update = lax.dot_general(
            p[:, :size], p, CONTRACT, precision=lax.Precision.HIGHEST, preferred_element_type=F32
        )
        left = m_ref[PANEL:, :] - update[PANEL:, :]
        m_ref[: size - PANEL, :size] = pltpu.roll(left[:, :size], size - PANEL, 1)
        m_ref[: size - PANEL, size:] = left[:, size:]
        return carry

    lax.fori_loop(0, size // PANEL, panel, 0)


def normalize(gram_matrix, vectors):
    size = gram_matrix.shape[0]
    inverse = call(
        inverse_kernel, [((size, size), F32)], 1, scratch=(pltpu.VMEM((size, 2 * size), F32),)
    )(gram_matrix)[0]
    return lax.dot_general(
        vectors,
        inverse,
        (((1,), (1,)), ((), ())),
        precision=lax.Precision.HIGHEST,
        preferred_element_type=F32,
    )


LINK = BF16


def per_device(start_block, locked_orbitals, cell_h):
    devices = lax.axis_size(AXES)
    nodes_total = float(
        start_block.shape[0] * start_block.shape[1] * start_block.shape[2] * devices
    )
    rim_x = passed_along(start_block[0:1], "gx", -1)
    low_y = jnp.concatenate([start_block[:, 0:1], rim_x[:, 0:1]], 0)
    rim_y = passed_along(low_y, "gy", -1)
    low_z = jnp.concatenate([start_block[:, :, 0], rim_x[:, :, 0]], 0)
    low_z = jnp.concatenate([low_z, rim_y[:, :, 0]], 1)
    rim_z = passed_along(low_z, "gz", -1)
    h = call(order_kernel, [((CELLS, CELL_OUT, CELL_IN), BF16)], 1, cost=4_000_000)(
        cell_h.reshape(CELLS, NODE, NODE)
    )[0]
    h = pltpu.with_memory_space_constraint(h, pltpu.VMEM)
    locked_flat = locked_orbitals.reshape(-1, LOCKED)
    wide = [locked_flat[:, i : i + 128] for i in range(0, LOCKED, 128)]
    blocks = [
        lax.dot_general(wide[j], wide[i], CONTRACT, preferred_element_type=F32)
        for i in range(3)
        for j in range(i, 3)
    ]
    locked_parts = jnp.concatenate(
        [jnp.concatenate(blocks[i : i + 2], 0) for i in (0, 2, 4)], 1
    )

    state = ((3 * ROWS, WIDTH), F32)
    fields = [state, ((208, WIDTH), LINK), ((208, WIDTH), LINK)]
    scratch = (pltpu.VMEM((ROWS, WIDTH), BF16),)
    odd = (lax.axis_index("gx") % 2).astype(jnp.int32).reshape(1)
    carry = call(first_kernel, fields, 5, scratch=scratch, scalars=1)(
        odd, start_block, rim_x, rim_y, rim_z, h
    )
    factors, sigma = [(SIGMA / HALF, 0.0)], SIGMA
    for repeat in range(APPLY - 1):
        following = 1.0 / (2.0 / SIGMA - sigma)
        factors.append((2.0 * following / HALF, sigma * following))
        sigma = following
    table = jnp.array(factors[:-1], F32).reshape(-1)

    def exchange(s, near, far):
        near, far = swapped(near, far)
        s, low, high = call(
            fold_x_kernel, [state] + [((176, WIDTH), LINK)] * 2, 3, aliases={1: 0}, scalars=1
        )(odd, s, near, far)
        below, above = both_ways(low, high, "gy")
        s, low, high = call(
            fold_y_kernel, [state] + [((PLANE, WIDTH), LINK)] * 2, 3, aliases={0: 0}
        )(s, below, above)
        below, above = both_ways(low, high, "gz")
        return s, below, above

    def apply(number, carry):
        index = jnp.asarray(number, jnp.int32).reshape(1)
        s, near, far = call(
            step_kernel, fields, 4, scratch=scratch, scalars=3, aliases={3: 0}
        )(odd, index, table, *exchange(*carry), h)
        return pltpu.with_memory_space_constraint(s, pltpu.VMEM), near, far

    carry = lax.fori_loop(1, APPLY - 1, apply, apply(0, carry))
    scale, shift = factors[-1]
    filtered, parts = call(
        functools.partial(last_kernel, scale, shift),
        [((864, WIDTH), BF16), ((256, 256), F32)],
        4,
        scratch=(pltpu.VMEM((ROWS, WIDTH), F32),),
    )(*exchange(*carry), locked_flat)
    total = mesh_total(jnp.concatenate([parts, locked_parts], 1))
    g = [total[r : r + 128, c : c + 128] for c in (256, 384, 512) for r in (0, 128)]
    locked_gram = jnp.concatenate(
        [
            jnp.concatenate([g[0], g[1].T, g[2].T], 1),
            jnp.concatenate([g[1], g[3], g[4].T], 1),
            jnp.concatenate([g[2], g[4], g[5]], 1),
        ],
        0,
    )
    self_gram = total[:128, :128]
    cross = jnp.concatenate([total[128:, :128], total[:128, 128:256], total[128:, 128:256]], 0)
    coefficient = (cross / nodes_total).astype(BF16)
    coef_wide = coefficient.astype(F32)
    projected = filtered.astype(F32) - jnp.dot(
        locked_flat, coefficient, preferred_element_type=F32
    )
    precise = dict(precision=lax.Precision.HIGHEST, preferred_element_type=F32)
    mixed = lax.dot_general(cross, coef_wide, CONTRACT, **precise)
    weighted = jnp.dot(locked_gram, coef_wide, **precise)
    quadratic = lax.dot_general(coef_wide, weighted, CONTRACT, **precise)
    gram_matrix = (self_gram - mixed - mixed.T + quadratic) / nodes_total
    result = normalize(gram_matrix, projected)
    return result.reshape(start_block.shape)


def solution(mesh):
    placed = (P("gx", "gy", "gz", None), P("gx", "gy", "gz", None), P("gx", "gy", "gz", None, None))
    return jax.shard_map(
        per_device, mesh=mesh, in_specs=placed, out_specs=P("gx", "gy", "gz", None), check_vma=False
    )
```

```python
import functools

import jax
import jax.numpy as jnp
from jax import lax
from jax.experimental import pallas as pl
from jax.experimental.pallas import tpu as pltpu
from jax.sharding import PartitionSpec as P


ORDER = 6
SIDE = 7
NODE = 343
APPLY = 6
LOCKED = 384
WIDTH = 128

PLANE = 56
CELLS = 4
LAYERS = 6 * CELLS + 1
ROWS = 1408
STEP = 6 * PLANE
CELL_OUT = SIDE * PLANE
CELL_IN = CELL_OUT + 8
ROOM = 36

filter_low = 3.0
filter_high = 40.0
filter_bottom = 0.5
HALF = (filter_high - filter_low) / 2.0
CENTER = (filter_high + filter_low) / 2.0
SIGMA = HALF / (filter_bottom - CENTER)

F32 = jnp.float32
BF16 = jnp.bfloat16
AXES = ("gx", "gy", "gz")
CONTRACT = (((0,), (0,)), ((), ()))
VM = pl.BlockSpec(memory_space=pltpu.VMEM)
SM = pl.BlockSpec(memory_space=pltpu.SMEM)


def call(kernel, outs, n_in, cost=1_000_000, scratch=(), aliases=None, scalars=0, far=0):
    return pl.pallas_call(
        kernel,
        out_shape=[jax.ShapeDtypeStruct(s, d) for s, d in outs],
        in_specs=[SM] * scalars + [VM] * n_in + [pl.BlockSpec(memory_space=pl.ANY)] * far,
        out_specs=[VM] * len(outs),
        scratch_shapes=list(scratch),
        input_output_aliases=aliases or {},
        compiler_params=pltpu.CompilerParams(vmem_limit_bytes=(48 if far else 16) * 2**20),
        cost_estimate=pl.CostEstimate(flops=cost, bytes_accessed=cost, transcendentals=0),
    )


def passed_along(block, axis, distance):
    devices = range(lax.axis_size(axis))
    route = [((i - distance) % len(devices), i) for i in devices]
    return lax.ppermute(block, axis, route)


def swapped(near, far):
    count = lax.axis_size("gx")
    partner = [(i, i ^ 1) for i in range(count)]
    across = [(i, (i + 2 * (i % 2) - 1) % count) for i in range(count)]
    return lax.ppermute(near, "gx", partner), lax.ppermute(far, "gx", across)


def both_ways(low_face, high_face, axis):
    return passed_along(high_face, axis, 1), passed_along(low_face, axis, -1)


def order_kernel(h_ref, out_ref):
    row = lax.broadcasted_iota(jnp.int32, (CELL_IN, NODE), 0)
    col = lax.broadcasted_iota(jnp.int32, (CELL_IN, NODE), 1)
    z, rest = row // PLANE, row % PLANE
    x, y = rest // 8, rest % 8
    pick = jnp.where((x * 49 + y * 7 + z == col) & (y < SIDE) & (z < SIDE), 1.0, 0.0).astype(BF16)
    half = jnp.dot(pick[:CELL_OUT], h_ref[0], preferred_element_type=F32).astype(BF16)
    out_ref[0] = lax.dot_general(
        half, pick, (((1,), (1,)), ((), ())), preferred_element_type=F32
    ).astype(BF16)


def ordered_cells(cell_h):
    return pl.pallas_call(
        order_kernel,
        grid=(CELLS,),
        in_specs=[pl.BlockSpec((1, NODE, NODE), lambda k: (k, 0, 0))],
        out_specs=pl.BlockSpec((1, CELL_OUT, CELL_IN), lambda k: (k, 0, 0)),
        out_shape=jax.ShapeDtypeStruct((ROOM, CELL_OUT, CELL_IN), BF16),
        compiler_params=pltpu.CompilerParams(vmem_limit_bytes=16 * 2**20),
        cost_estimate=pl.CostEstimate(
            flops=4_000_000, bytes_accessed=4_000_000, transcendentals=0
        ),
    )(cell_h)


def streamed(h_hbm, h_ref, sems):
    copies = [pltpu.make_async_copy(h_hbm.at[k], h_ref.at[k], sems.at[k]) for k in range(CELLS)]
    for copy in copies:
        copy.start()
    return copies


def multiply(odd_ref, copies, h_ref, w_ref, near_ref, far_ref, v_ref):
    for k in range(CELLS):
        copies[k].wait()
        y = jnp.dot(h_ref[k], v_ref[k * STEP : k * STEP + CELL_IN, :], preferred_element_type=F32)
        if k:
            w_ref[k * STEP : k * STEP + PLANE, :] += y[:PLANE]
        else:
            w_ref[:PLANE, :] = y[:PLANE]
        w_ref[k * STEP + PLANE : k * STEP + CELL_OUT, :] = y[PLANE:]
    w_ref[LAYERS * PLANE : ROWS, :] = jnp.zeros((ROWS - LAYERS * PLANE, WIDTH), F32)
    odd = odd_ref[0] == 1
    low, high = (
        jnp.concatenate(
            [w_ref[z * PLANE + x * 8 : z * PLANE + x * 8 + 8, :] for z in range(LAYERS)]
            + [jnp.zeros((8, WIDTH), F32)],
            0,
        )
        for x in (0, ORDER)
    )
    near_ref[...] = jnp.where(odd, low, high).astype(near_ref.dtype)
    far_ref[...] = jnp.where(odd, high, low).astype(far_ref.dtype)


def box(number):
    return pl.multiple_of((1 + number % 2) * ROWS, ROWS)


def first_kernel(
    odd_ref, start_ref, x_ref, y_ref, z_ref, h_hbm, s_ref, near_ref, far_ref, v_ref, h_ref, sems
):
    copies = streamed(h_hbm, h_ref, sems)
    s_ref[ROWS:, :] = jnp.zeros((2 * ROWS, WIDTH), F32)
    for x in range(SIDE):
        for y in range(SIDE):
            if x < 6 and y < 6:
                line = start_ref[x, y]
            elif y < 6:
                line = x_ref[0, y]
            else:
                line = y_ref[x, 0]
            s_ref[pl.ds(ROWS + x * 8 + y, LAYERS - 1, stride=PLANE), :] = line.astype(F32)
        top = ROWS + (LAYERS - 1) * PLANE + x * 8
        s_ref[top : top + SIDE, :] = z_ref[x].astype(F32)
    for begin, size in CHUNKS:
        v_ref[begin : begin + size, :] = s_ref[ROWS + begin : ROWS + begin + size, :].astype(BF16)
    multiply(odd_ref, copies, h_ref, s_ref, near_ref, far_ref, v_ref)


CHUNKS = [(i * 112, 112) for i in range(12)] + [(1344, 64)]


def recur(scale, shift, s_ref, below_ref, above_ref, now, old, begin, size):
    w = s_ref[begin : begin + size, :]
    for at, face_ref in ((0, below_ref), (CHUNKS[-1][0], above_ref)):
        if begin == at:
            rest = jnp.zeros((size - PLANE, WIDTH), F32)
            w = w + jnp.concatenate([face_ref[...].astype(F32), rest], 0)
    out = scale * (w - CENTER * s_ref[pl.ds(now + begin, size), :])
    return out - shift * s_ref[pl.ds(old + begin, size), :]


def step_kernel(
    odd_ref, index_ref, factor_ref, s_in, below, above, h_hbm, s_ref, near_ref, far_ref, v_ref, h_ref, sems
):
    copies = streamed(h_hbm, h_ref, sems)
    number = index_ref[0]
    scale, shift = factor_ref[2 * number], factor_ref[2 * number + 1]
    now, old = box(number), box(number + 1)
    for begin, size in CHUNKS:
        out = recur(scale, shift, s_in, below, above, now, old, begin, size)
        s_ref[pl.ds(old + begin, size), :] = out
        v_ref[begin : begin + size, :] = out.astype(BF16)
    multiply(odd_ref, copies, h_ref, s_ref, near_ref, far_ref, v_ref)


def fold_x_kernel(odd_ref, w_in, near_ref, far_ref, w_ref, low_ref, high_ref):
    odd = odd_ref[0] == 1
    for z in range(LAYERS):
        near = near_ref[z * 8 : z * 8 + 8, :].astype(F32)
        far = far_ref[z * 8 : z * 8 + 8, :].astype(F32)
        for x, add in ((0, jnp.where(odd, near, far)), (ORDER, jnp.where(odd, far, near))):
            rows = slice(z * PLANE + x * 8, z * PLANE + x * 8 + 8)
            w_ref[rows, :] += add
    lines = LAYERS * SIDE
    for ref, y in ((low_ref, 0), (high_ref, ORDER)):
        face = w_ref[pl.ds(y, lines, stride=8), :]
        ref[...] = jnp.concatenate([face, jnp.zeros((1, WIDTH), F32)], 0).astype(ref.dtype)


def fold_y_kernel(w_in, below_ref, above_ref, w_ref, low_ref, high_ref):
    lines = LAYERS * SIDE
    for ref, y in ((below_ref, 0), (above_ref, ORDER)):
        rows = pl.ds(y, lines, stride=8)
        w_ref[rows, :] = w_ref[rows, :] + ref[...].astype(F32)[:lines]
    low_ref[...] = w_ref[:PLANE, :].astype(low_ref.dtype)
    high_ref[...] = w_ref[(LAYERS - 1) * PLANE : LAYERS * PLANE, :].astype(high_ref.dtype)


def last_kernel(scale, shift, s_ref, below, above, locked_ref, filtered_ref, parts_ref, field):
    now, old = (ROWS * (1 + (number % 2)) for number in (APPLY - 1, APPLY))
    for begin, size in CHUNKS:
        field[begin : begin + size, :] = recur(
            scale, shift, s_ref, below, above, now, old, begin, size
        )
    depth = LAYERS - 1
    for x in range(ORDER):
        for y in range(ORDER):
            at = (x * ORDER + y) * depth
            line = field[pl.ds(x * 8 + y, depth, stride=PLANE), :]
            filtered_ref[at : at + depth, :] = line.astype(BF16)
    f = filtered_ref[...]
    parts_ref[:128, :128] = lax.dot_general(f, f, CONTRACT, preferred_element_type=F32)
    for i, (r, c) in enumerate(((128, 0), (0, 128), (128, 128))):
        parts_ref[r : r + 128, c : c + 128] = lax.dot_general(
            locked_ref[:, i * 128 : i * 128 + 128], f, CONTRACT, preferred_element_type=F32
        )


def mesh_total(rows):
    odd = lax.axis_index("gx") % 2 == 1
    count = lax.axis_size("gx")
    partner = [(i, i ^ 1) for i in range(count)]
    lower, upper = jnp.split(rows, 2)
    other = lax.ppermute(jnp.where(odd, lower, upper), "gx", partner)
    half = jnp.where(odd, upper, lower) + other
    axes = ("gy", "gz")
    pieces = half.reshape(lax.axis_size(axes), -1, rows.shape[1])
    mine = lax.all_to_all(pieces, axes, 0, 0).sum(0)
    total = mine
    for step in range(2, count, 2):
        total = total + passed_along(mine, "gx", step)
    half = lax.all_to_all(jnp.broadcast_to(total, pieces.shape), axes, 0, 0).reshape(half.shape)
    other = lax.ppermute(half, "gx", partner)
    return jnp.concatenate([jnp.where(odd, other, half), jnp.where(odd, half, other)], 0)


PANEL = 16
PIVOTS = 8


def inverse_kernel(a_ref, out_ref, m_ref):
    size = a_ref.shape[0]
    m_ref[:, :size] = a_ref[...]
    r = lax.broadcasted_iota(jnp.int32, (size, size), 0)
    c = lax.broadcasted_iota(jnp.int32, (size, size), 1)
    m_ref[:, size:] = jnp.where(r == c, 1.0, 0.0)
    line = lax.broadcasted_iota(jnp.int32, (PANEL, 2 * size), 0)

    def panel(step, carry):
        p = m_ref[:PANEL, :]
        scale = jnp.ones((PANEL, 2 * size), F32)
        for i in range(0, PANEL, PIVOTS):
            span = range(PIVOTS)
            rows = [jnp.broadcast_to(p[i + u : i + u + 1, :], p.shape) for u in span]
            cols = [jnp.broadcast_to(p[:, i + u : i + u + 1], p.shape) for u in span]
            s = [
                [jnp.broadcast_to(rows[u][:, i + v : i + v + 1], p.shape) for v in span]
                for u in span
            ]
            for u in span:
                inv = 1.0 / s[u][u]
                scale = jnp.where(line == i + u, lax.rsqrt(s[u][u]), scale)
                for v in range(u + 1, PIVOTS):
                    f = s[u][v] * inv
                    rows[v] = rows[v] - f * rows[u]
                    cols[v] = cols[v] - f * cols[u]
                    for w in range(v, PIVOTS):
                        s[v][w] = s[v][w] - f * s[u][w]
                cols[u] = cols[u] * inv
            new = p
            for u in span:
                new = new - cols[u] * rows[u]
            p = jnp.where(line >= i + PIVOTS, new, p)
            for u in span:
                p = jnp.where(line == i + u, rows[u], p)
        p = p * scale
        out_ref[pl.ds(pl.multiple_of(step * PANEL, PANEL), PANEL), :] = p[:, size:]
        update = lax.dot_general(
            p[:, :size], p, CONTRACT, precision=lax.Precision.HIGHEST, preferred_element_type=F32
        )
        left = m_ref[PANEL:, :] - update[PANEL:, :]
        m_ref[: size - PANEL, :size] = pltpu.roll(left[:, :size], size - PANEL, 1)
        m_ref[: size - PANEL, size:] = left[:, size:]
        return carry

    lax.fori_loop(0, size // PANEL, panel, 0)


def normalize(gram_matrix, vectors):
    size = gram_matrix.shape[0]
    inverse = call(
        inverse_kernel, [((size, size), F32)], 1, scratch=(pltpu.VMEM((size, 2 * size), F32),)
    )(gram_matrix)[0]
    return lax.dot_general(
        vectors,
        inverse,
        (((1,), (1,)), ((), ())),
        precision=lax.Precision.HIGHEST,
        preferred_element_type=F32,
    )


LINK = BF16


def per_device(start_block, locked_orbitals, cell_h):
    devices = lax.axis_size(AXES)
    nodes_total = float(
        start_block.shape[0] * start_block.shape[1] * start_block.shape[2] * devices
    )
    rim_x = passed_along(start_block[0:1], "gx", -1)
    low_y = jnp.concatenate([start_block[:, 0:1], rim_x[:, 0:1]], 0)
    rim_y = passed_along(low_y, "gy", -1)
    low_z = jnp.concatenate([start_block[:, :, 0], rim_x[:, :, 0]], 0)
    low_z = jnp.concatenate([low_z, rim_y[:, :, 0]], 1)
    rim_z = passed_along(low_z, "gz", -1)
    h = ordered_cells(cell_h.reshape(CELLS, NODE, NODE))
    locked_flat = locked_orbitals.reshape(-1, LOCKED)
    wide = [locked_flat[:, i : i + 128] for i in range(0, LOCKED, 128)]
    blocks = [
        lax.dot_general(wide[j], wide[i], CONTRACT, preferred_element_type=F32)
        for i in range(3)
        for j in range(i, 3)
    ]
    locked_parts = jnp.concatenate(
        [jnp.concatenate(blocks[i : i + 2], 0) for i in (0, 2, 4)], 1
    )

    state = ((3 * ROWS, WIDTH), F32)
    fields = [state, ((208, WIDTH), LINK), ((208, WIDTH), LINK)]
    scratch = (
        pltpu.VMEM((ROWS, WIDTH), BF16),
        pltpu.VMEM((CELLS, CELL_OUT, CELL_IN), BF16),
        pltpu.SemaphoreType.DMA((CELLS,)),
    )
    odd = (lax.axis_index("gx") % 2).astype(jnp.int32).reshape(1)
    carry = call(first_kernel, fields, 4, scratch=scratch, scalars=1, far=1)(
        odd, start_block, rim_x, rim_y, rim_z, h
    )
    factors, sigma = [(SIGMA / HALF, 0.0)], SIGMA
    for repeat in range(APPLY - 1):
        following = 1.0 / (2.0 / SIGMA - sigma)
        factors.append((2.0 * following / HALF, sigma * following))
        sigma = following
    table = jnp.array(factors[:-1], F32).reshape(-1)

    def exchange(s, near, far):
        near, far = swapped(near, far)
        s, low, high = call(
            fold_x_kernel, [state] + [((176, WIDTH), LINK)] * 2, 3, aliases={1: 0}, scalars=1
        )(odd, s, near, far)
        below, above = both_ways(low, high, "gy")
        s, low, high = call(
            fold_y_kernel, [state] + [((PLANE, WIDTH), LINK)] * 2, 3, aliases={0: 0}
        )(s, below, above)
        below, above = both_ways(low, high, "gz")
        return s, below, above

    def apply(number, carry):
        index = jnp.asarray(number, jnp.int32).reshape(1)
        s, near, far = call(
            step_kernel, fields, 3, scratch=scratch, scalars=3, aliases={3: 0}, far=1
        )(odd, index, table, *exchange(*carry), h)
        return pltpu.with_memory_space_constraint(s, pltpu.VMEM), near, far

    carry = lax.fori_loop(1, APPLY - 1, apply, apply(0, carry))
    scale, shift = factors[-1]
    filtered, parts = call(
        functools.partial(last_kernel, scale, shift),
        [((864, WIDTH), BF16), ((256, 256), F32)],
        4,
        scratch=(pltpu.VMEM((ROWS, WIDTH), F32),),
    )(*exchange(*carry), locked_flat)
    total = mesh_total(jnp.concatenate([parts, locked_parts], 1))
    g = [total[r : r + 128, c : c + 128] for c in (256, 384, 512) for r in (0, 128)]
    locked_gram = jnp.concatenate(
        [
            jnp.concatenate([g[0], g[1].T, g[2].T], 1),
            jnp.concatenate([g[1], g[3], g[4].T], 1),
            jnp.concatenate([g[2], g[4], g[5]], 1),
        ],
        0,
    )
    self_gram = total[:128, :128]
    cross = jnp.concatenate([total[128:, :128], total[:128, 128:256], total[128:, 128:256]], 0)
    coefficient = (cross / nodes_total).astype(BF16)
    coef_wide = coefficient.astype(F32)
    projected = filtered.astype(F32) - jnp.dot(
        locked_flat, coefficient, preferred_element_type=F32
    )
    precise = dict(precision=lax.Precision.HIGHEST, preferred_element_type=F32)
    mixed = lax.dot_general(cross, coef_wide, CONTRACT, **precise)
    weighted = jnp.dot(locked_gram, coef_wide, **precise)
    quadratic = lax.dot_general(coef_wide, weighted, CONTRACT, **precise)
    gram_matrix = (self_gram - mixed - mixed.T + quadratic) / nodes_total
    result = normalize(gram_matrix, projected)
    return result.reshape(start_block.shape)


def solution(mesh):
    placed = (P("gx", "gy", "gz", None), P("gx", "gy", "gz", None), P("gx", "gy", "gz", None, None))
    return jax.shard_map(
        per_device, mesh=mesh, in_specs=placed, out_specs=P("gx", "gy", "gz", None), check_vma=False
    )
```

```python
import functools

import jax
import jax.numpy as jnp
from jax import lax
from jax.experimental import pallas as pl
from jax.experimental.pallas import tpu as pltpu
from jax.sharding import PartitionSpec as P


ORDER = 6
SIDE = 7
NODE = 343
APPLY = 6
LOCKED = 384
WIDTH = 128

PLANE = 56
CELLS = 4
LAYERS = 6 * CELLS + 1
ROWS = 1408
STEP = 6 * PLANE
CELL_OUT = SIDE * PLANE
CELL_IN = CELL_OUT + 8

filter_low = 3.0
filter_high = 40.0
filter_bottom = 0.5
HALF = (filter_high - filter_low) / 2.0
CENTER = (filter_high + filter_low) / 2.0
SIGMA = HALF / (filter_bottom - CENTER)

F32 = jnp.float32
BF16 = jnp.bfloat16
AXES = ("gx", "gy", "gz")
CONTRACT = (((0,), (0,)), ((), ()))
PARAMS = pltpu.CompilerParams(vmem_limit_bytes=16 * 2**20)
VM = pl.BlockSpec(memory_space=pltpu.VMEM)
SM = pl.BlockSpec(memory_space=pltpu.SMEM)


def call(kernel, outs, n_in, cost=1_000_000, scratch=(), aliases=None, scalars=0):
    return pl.pallas_call(
        kernel,
        out_shape=[jax.ShapeDtypeStruct(s, d) for s, d in outs],
        in_specs=[SM] * scalars + [VM] * n_in,
        out_specs=[VM] * len(outs),
        scratch_shapes=list(scratch),
        input_output_aliases=aliases or {},
        compiler_params=PARAMS,
        cost_estimate=pl.CostEstimate(flops=cost, bytes_accessed=cost, transcendentals=0),
    )


def passed_along(block, axis, distance):
    devices = range(lax.axis_size(axis))
    route = [((i - distance) % len(devices), i) for i in devices]
    return lax.ppermute(block, axis, route)


def swapped(near, far):
    count = lax.axis_size("gx")
    partner = [(i, i ^ 1) for i in range(count)]
    across = [(i, (i + 2 * (i % 2) - 1) % count) for i in range(count)]
    return lax.ppermute(near, "gx", partner), lax.ppermute(far, "gx", across)


def both_ways(low_face, high_face, axis):
    return passed_along(high_face, axis, 1), passed_along(low_face, axis, -1)


def order_kernel(h_ref, out_ref):
    row = lax.broadcasted_iota(jnp.int32, (CELL_IN, NODE), 0)
    col = lax.broadcasted_iota(jnp.int32, (CELL_IN, NODE), 1)
    z, rest = row // PLANE, row % PLANE
    x, y = rest // 8, rest % 8
    pick = jnp.where((x * 49 + y * 7 + z == col) & (y < SIDE) & (z < SIDE), 1.0, 0.0).astype(BF16)
    for k in range(CELLS):
        half = jnp.dot(pick[:CELL_OUT], h_ref[k], preferred_element_type=F32).astype(BF16)
        out_ref[k] = lax.dot_general(
            half, pick, (((1,), (1,)), ((), ())), preferred_element_type=F32
        ).astype(BF16)


def multiply(odd_ref, h_ref, w_ref, near_ref, far_ref, v_ref):
    for k in range(CELLS):
        y = jnp.dot(h_ref[k], v_ref[k * STEP : k * STEP + CELL_IN, :], preferred_element_type=F32)
        if k:
            w_ref[k * STEP : k * STEP + PLANE, :] += y[:PLANE]
        else:
            w_ref[:PLANE, :] = y[:PLANE]
        w_ref[k * STEP + PLANE : k * STEP + CELL_OUT, :] = y[PLANE:]
    w_ref[LAYERS * PLANE : ROWS, :] = jnp.zeros((ROWS - LAYERS * PLANE, WIDTH), F32)
    odd = odd_ref[0] == 1
    low, high = (
        jnp.concatenate(
            [w_ref[z * PLANE + x * 8 : z * PLANE + x * 8 + 8, :] for z in range(LAYERS)]
            + [jnp.zeros((8, WIDTH), F32)],
            0,
        )
        for x in (0, ORDER)
    )
    near_ref[...] = jnp.where(odd, low, high).astype(near_ref.dtype)
    far_ref[...] = jnp.where(odd, high, low).astype(far_ref.dtype)


def box(number):
    return pl.multiple_of((1 + number % 2) * ROWS, ROWS)


def first_kernel(odd_ref, start_ref, x_ref, y_ref, z_ref, h_ref, s_ref, near_ref, far_ref, v_ref):
    s_ref[ROWS:, :] = jnp.zeros((2 * ROWS, WIDTH), F32)
    for x in range(SIDE):
        for y in range(SIDE):
            if x < 6 and y < 6:
                line = start_ref[x, y]
            elif y < 6:
                line = x_ref[0, y]
            else:
                line = y_ref[x, 0]
            s_ref[pl.ds(ROWS + x * 8 + y, LAYERS - 1, stride=PLANE), :] = line.astype(F32)
        top = ROWS + (LAYERS - 1) * PLANE + x * 8
        s_ref[top : top + SIDE, :] = z_ref[x].astype(F32)
    for begin, size in CHUNKS:
        v_ref[begin : begin + size, :] = s_ref[ROWS + begin : ROWS + begin + size, :].astype(BF16)
    multiply(odd_ref, h_ref, s_ref, near_ref, far_ref, v_ref)


CHUNKS = [(i * 112, 112) for i in range(12)] + [(1344, 64)]


def recur(scale, shift, s_ref, below_ref, above_ref, now, old, begin, size):
    w = s_ref[begin : begin + size, :]
    for at, face_ref in ((0, below_ref), (CHUNKS[-1][0], above_ref)):
        if begin == at:
            rest = jnp.zeros((size - PLANE, WIDTH), F32)
            w = w + jnp.concatenate([face_ref[...].astype(F32), rest], 0)
    out = scale * (w - CENTER * s_ref[pl.ds(now + begin, size), :])
    return out - shift * s_ref[pl.ds(old + begin, size), :]


def step_kernel(
    odd_ref, index_ref, factor_ref, s_in, below, above, h_ref, s_ref, near_ref, far_ref, v_ref
):
    number = index_ref[0]
    scale, shift = factor_ref[2 * number], factor_ref[2 * number + 1]
    now, old = box(number), box(number + 1)
    for begin, size in CHUNKS:
        out = recur(scale, shift, s_in, below, above, now, old, begin, size)
        s_ref[pl.ds(old + begin, size), :] = out
        v_ref[begin : begin + size, :] = out.astype(BF16)
    multiply(odd_ref, h_ref, s_ref, near_ref, far_ref, v_ref)


def fold_x_kernel(odd_ref, w_in, near_ref, far_ref, w_ref, low_ref, high_ref):
    odd = odd_ref[0] == 1
    for z in range(LAYERS):
        near = near_ref[z * 8 : z * 8 + 8, :].astype(F32)
        far = far_ref[z * 8 : z * 8 + 8, :].astype(F32)
        for x, add in ((0, jnp.where(odd, near, far)), (ORDER, jnp.where(odd, far, near))):
            rows = slice(z * PLANE + x * 8, z * PLANE + x * 8 + 8)
            w_ref[rows, :] += add
    lines = LAYERS * SIDE
    for ref, y in ((low_ref, 0), (high_ref, ORDER)):
        face = w_ref[pl.ds(y, lines, stride=8), :]
        ref[...] = jnp.concatenate([face, jnp.zeros((1, WIDTH), F32)], 0).astype(ref.dtype)


def fold_y_kernel(w_in, below_ref, above_ref, w_ref, low_ref, high_ref):
    lines = LAYERS * SIDE
    for ref, y in ((below_ref, 0), (above_ref, ORDER)):
        rows = pl.ds(y, lines, stride=8)
        w_ref[rows, :] = w_ref[rows, :] + ref[...].astype(F32)[:lines]
    low_ref[...] = w_ref[:PLANE, :].astype(low_ref.dtype)
    high_ref[...] = w_ref[(LAYERS - 1) * PLANE : LAYERS * PLANE, :].astype(high_ref.dtype)


def last_kernel(scale, shift, s_ref, below, above, locked_ref, filtered_ref, parts_ref, field):
    now, old = (ROWS * (1 + (number % 2)) for number in (APPLY - 1, APPLY))
    for begin, size in CHUNKS:
        field[begin : begin + size, :] = recur(
            scale, shift, s_ref, below, above, now, old, begin, size
        )
    depth = LAYERS - 1
    for x in range(ORDER):
        for y in range(ORDER):
            at = (x * ORDER + y) * depth
            line = field[pl.ds(x * 8 + y, depth, stride=PLANE), :]
            filtered_ref[at : at + depth, :] = line.astype(BF16)
    f = filtered_ref[...]
    parts_ref[:128, :128] = lax.dot_general(f, f, CONTRACT, preferred_element_type=F32)
    for i, (r, c) in enumerate(((128, 0), (0, 128), (128, 128))):
        parts_ref[r : r + 128, c : c + 128] = lax.dot_general(
            locked_ref[:, i * 128 : i * 128 + 128], f, CONTRACT, preferred_element_type=F32
        )


def mesh_total(rows):
    odd = lax.axis_index("gx") % 2 == 1
    count = lax.axis_size("gx")
    partner = [(i, i ^ 1) for i in range(count)]
    lower, upper = jnp.split(rows, 2)
    other = lax.ppermute(jnp.where(odd, lower, upper), "gx", partner)
    half = jnp.where(odd, upper, lower) + other
    axes = ("gy", "gz")
    pieces = half.reshape(lax.axis_size(axes), -1, rows.shape[1])
    mine = lax.all_to_all(pieces, axes, 0, 0).sum(0)
    total = mine
    for step in range(2, count, 2):
        total = total + passed_along(mine, "gx", step)
    half = lax.all_to_all(jnp.broadcast_to(total, pieces.shape), axes, 0, 0).reshape(half.shape)
    other = lax.ppermute(half, "gx", partner)
    return jnp.concatenate([jnp.where(odd, other, half), jnp.where(odd, half, other)], 0)


PANEL = 16
PIVOTS = 8


def inverse_kernel(a_ref, out_ref, m_ref):
    size = a_ref.shape[0]
    m_ref[:, :size] = a_ref[...]
    r = lax.broadcasted_iota(jnp.int32, (size, size), 0)
    c = lax.broadcasted_iota(jnp.int32, (size, size), 1)
    m_ref[:, size:] = jnp.where(r == c, 1.0, 0.0)
    line = lax.broadcasted_iota(jnp.int32, (PANEL, 2 * size), 0)

    def panel(step, carry):
        p = m_ref[:PANEL, :]
        scale = jnp.ones((PANEL, 2 * size), F32)
        for i in range(0, PANEL, PIVOTS):
            span = range(PIVOTS)
            rows = [jnp.broadcast_to(p[i + u : i + u + 1, :], p.shape) for u in span]
            cols = [jnp.broadcast_to(p[:, i + u : i + u + 1], p.shape) for u in span]
            s = [
                [jnp.broadcast_to(rows[u][:, i + v : i + v + 1], p.shape) for v in span]
                for u in span
            ]
            for u in span:
                inv = 1.0 / s[u][u]
                scale = jnp.where(line == i + u, lax.rsqrt(s[u][u]), scale)
                for v in range(u + 1, PIVOTS):
                    f = s[u][v] * inv
                    rows[v] = rows[v] - f * rows[u]
                    cols[v] = cols[v] - f * cols[u]
                    for w in range(v, PIVOTS):
                        s[v][w] = s[v][w] - f * s[u][w]
                cols[u] = cols[u] * inv
            new = p
            for u in span:
                new = new - cols[u] * rows[u]
            p = jnp.where(line >= i + PIVOTS, new, p)
            for u in span:
                p = jnp.where(line == i + u, rows[u], p)
        p = p * scale
        out_ref[pl.ds(pl.multiple_of(step * PANEL, PANEL), PANEL), :] = p[:, size:]
        update = lax.dot_general(
            p[:, :size], p, CONTRACT, precision=lax.Precision.HIGHEST, preferred_element_type=F32
        )
        left = m_ref[PANEL:, :] - update[PANEL:, :]
        m_ref[: size - PANEL, :size] = pltpu.roll(left[:, :size], size - PANEL, 1)
        m_ref[: size - PANEL, size:] = left[:, size:]
        return carry

    lax.fori_loop(0, size // PANEL, panel, 0)


def normalize(gram_matrix, vectors):
    size = gram_matrix.shape[0]
    inverse = call(
        inverse_kernel, [((size, size), F32)], 1, scratch=(pltpu.VMEM((size, 2 * size), F32),)
    )(gram_matrix)[0]
    return lax.dot_general(
        vectors,
        inverse,
        (((1,), (1,)), ((), ())),
        precision=lax.Precision.HIGHEST,
        preferred_element_type=F32,
    )


LINK = BF16


def per_device(start_block, locked_orbitals, cell_h):
    devices = lax.axis_size(AXES)
    nodes_total = float(
        start_block.shape[0] * start_block.shape[1] * start_block.shape[2] * devices
    )
    rim_x = passed_along(start_block[0:1], "gx", -1)
    low_y = jnp.concatenate([start_block[:, 0:1], rim_x[:, 0:1]], 0)
    rim_y = passed_along(low_y, "gy", -1)
    low_z = jnp.concatenate([start_block[:, :, 0], rim_x[:, :, 0]], 0)
    low_z = jnp.concatenate([low_z, rim_y[:, :, 0]], 1)
    rim_z = passed_along(low_z, "gz", -1)
    h = call(order_kernel, [((CELLS, CELL_OUT, CELL_IN), BF16)], 1, cost=4_000_000)(
        cell_h.reshape(CELLS, NODE, NODE)
    )[0]
    h = pltpu.with_memory_space_constraint(h, pltpu.VMEM)
    locked_flat = locked_orbitals.reshape(-1, LOCKED)
    wide = [locked_flat[:, i : i + 128] for i in range(0, LOCKED, 128)]
    blocks = [
        lax.dot_general(wide[j], wide[i], CONTRACT, preferred_element_type=F32)
        for i in range(3)
        for j in range(i, 3)
    ]
    locked_parts = jnp.concatenate(
        [jnp.concatenate(blocks[i : i + 2], 0) for i in (0, 2, 4)], 1
    )

    state = ((3 * ROWS, WIDTH), F32)
    fields = [state, ((208, WIDTH), LINK), ((208, WIDTH), LINK)]
    scratch = (pltpu.VMEM((ROWS, WIDTH), BF16),)
    odd = (lax.axis_index("gx") % 2).astype(jnp.int32).reshape(1)
    carry = call(first_kernel, fields, 5, scratch=scratch, scalars=1)(
        odd, start_block, rim_x, rim_y, rim_z, h
    )
    factors, sigma = [(SIGMA / HALF, 0.0)], SIGMA
    for repeat in range(APPLY - 1):
        following = 1.0 / (2.0 / SIGMA - sigma)
        factors.append((2.0 * following / HALF, sigma * following))
        sigma = following
    table = jnp.array(factors[:-1], F32).reshape(-1)

    def exchange(s, near, far):
        near, far = swapped(near, far)
        s, low, high = call(
            fold_x_kernel, [state] + [((176, WIDTH), LINK)] * 2, 3, aliases={1: 0}, scalars=1
        )(odd, s, near, far)
        below, above = both_ways(low, high, "gy")
        s, low, high = call(
            fold_y_kernel, [state] + [((PLANE, WIDTH), LINK)] * 2, 3, aliases={0: 0}
        )(s, below, above)
        below, above = both_ways(low, high, "gz")
        return s, below, above

    def apply(number, carry):
        index = jnp.asarray(number, jnp.int32).reshape(1)
        s, near, far = call(
            step_kernel, fields, 4, scratch=scratch, scalars=3, aliases={3: 0}
        )(odd, index, table, *exchange(*carry), h)
        return pltpu.with_memory_space_constraint(s, pltpu.VMEM), near, far

    carry = lax.fori_loop(1, APPLY - 1, apply, apply(0, carry))
    scale, shift = factors[-1]
    filtered, parts = call(
        functools.partial(last_kernel, scale, shift),
        [((864, WIDTH), BF16), ((256, 256), F32)],
        4,
        scratch=(pltpu.VMEM((ROWS, WIDTH), F32),),
    )(*exchange(*carry), locked_flat)
    total = mesh_total(jnp.concatenate([parts, locked_parts], 1))
    g = [total[r : r + 128, c : c + 128] for c in (256, 384, 512) for r in (0, 128)]
    locked_gram = jnp.concatenate(
        [
            jnp.concatenate([g[0], g[1].T, g[2].T], 1),
            jnp.concatenate([g[1], g[3], g[4].T], 1),
            jnp.concatenate([g[2], g[4], g[5]], 1),
        ],
        0,
    )
    self_gram = total[:128, :128]
    cross = jnp.concatenate([total[128:, :128], total[:128, 128:256], total[128:, 128:256]], 0)
    coefficient = (cross / nodes_total).astype(BF16)
    coef_wide = coefficient.astype(F32)
    projected = filtered.astype(F32) - jnp.dot(
        locked_flat, coefficient, preferred_element_type=F32
    )
    precise = dict(precision=lax.Precision.HIGHEST, preferred_element_type=F32)
    mixed = lax.dot_general(cross, coef_wide, CONTRACT, **precise)
    weighted = jnp.dot(locked_gram, coef_wide, **precise)
    quadratic = lax.dot_general(coef_wide, weighted, CONTRACT, **precise)
    gram_matrix = (self_gram - mixed - mixed.T + quadratic) / nodes_total
    result = normalize(gram_matrix, projected)
    return result.reshape(start_block.shape)


def solution(mesh):
    placed = (P("gx", "gy", "gz", None), P("gx", "gy", "gz", None), P("gx", "gy", "gz", None, None))
    return jax.shard_map(
        per_device, mesh=mesh, in_specs=placed, out_specs=P("gx", "gy", "gz", None), check_vma=False
    )
```

```python
import functools

import jax
import jax.numpy as jnp
from jax import lax
from jax.experimental import pallas as pl
from jax.experimental.pallas import tpu as pltpu
from jax.sharding import PartitionSpec as P


ORDER = 6
SIDE = 7
NODE = 343
APPLY = 6
LOCKED = 384
WIDTH = 128

PLANE = 56
CELLS = 4
LAYERS = 6 * CELLS + 1
ROWS = 1408
STEP = 6 * PLANE
CELL_OUT = SIDE * PLANE
CELL_IN = CELL_OUT + 8

filter_low = 3.0
filter_high = 40.0
filter_bottom = 0.5
HALF = (filter_high - filter_low) / 2.0
CENTER = (filter_high + filter_low) / 2.0
SIGMA = HALF / (filter_bottom - CENTER)

F32 = jnp.float32
BF16 = jnp.bfloat16
AXES = ("gx", "gy", "gz")
CONTRACT = (((0,), (0,)), ((), ()))
PARAMS = pltpu.CompilerParams(vmem_limit_bytes=16 * 2**20)
VM = pl.BlockSpec(memory_space=pltpu.VMEM)
SM = pl.BlockSpec(memory_space=pltpu.SMEM)


def call(kernel, outs, n_in, cost=1_000_000, scratch=(), aliases=None, scalars=0):
    return pl.pallas_call(
        kernel,
        out_shape=[jax.ShapeDtypeStruct(s, d) for s, d in outs],
        in_specs=[SM] * scalars + [VM] * n_in,
        out_specs=[VM] * len(outs),
        scratch_shapes=list(scratch),
        input_output_aliases=aliases or {},
        compiler_params=PARAMS,
        cost_estimate=pl.CostEstimate(flops=cost, bytes_accessed=cost, transcendentals=0),
    )


def passed_along(block, axis, distance):
    devices = range(lax.axis_size(axis))
    route = [((i - distance) % len(devices), i) for i in devices]
    return lax.ppermute(block, axis, route)


def swapped(near, far):
    count = lax.axis_size("gx")
    partner = [(i, i ^ 1) for i in range(count)]
    across = [(i, (i + 2 * (i % 2) - 1) % count) for i in range(count)]
    return lax.ppermute(near, "gx", partner), lax.ppermute(far, "gx", across)


def both_ways(low_face, high_face, axis):
    return passed_along(high_face, axis, 1), passed_along(low_face, axis, -1)


def order_kernel(h_ref, out_ref):
    row = lax.broadcasted_iota(jnp.int32, (CELL_IN, NODE), 0)
    col = lax.broadcasted_iota(jnp.int32, (CELL_IN, NODE), 1)
    z, rest = row // PLANE, row % PLANE
    x, y = rest // 8, rest % 8
    pick = jnp.where((x * 49 + y * 7 + z == col) & (y < SIDE) & (z < SIDE), 1.0, 0.0).astype(BF16)
    for k in range(CELLS):
        half = jnp.dot(pick[:CELL_OUT], h_ref[k], preferred_element_type=F32).astype(BF16)
        out_ref[k] = lax.dot_general(
            half, pick, (((1,), (1,)), ((), ())), preferred_element_type=F32
        ).astype(BF16)


def multiply(odd_ref, h_ref, w_ref, near_ref, far_ref, v_ref):
    planes, top = [], None
    for k in range(CELLS):
        y = jnp.dot(h_ref[k], v_ref[k * STEP : k * STEP + CELL_IN, :], preferred_element_type=F32)
        pieces = [y[j * PLANE : (j + 1) * PLANE] for j in range(SIDE)]
        if top is not None:
            pieces[0] = pieces[0] + top
        top = pieces.pop()
        if k == CELLS - 1:
            pieces.append(top)
        for piece in pieces:
            at = len(planes) * PLANE
            w_ref[at : at + PLANE, :] = piece
            planes.append((piece[:8], piece[ORDER * 8 :]))
    w_ref[LAYERS * PLANE : ROWS, :] = jnp.zeros((ROWS - LAYERS * PLANE, WIDTH), F32)
    odd = odd_ref[0] == 1
    pad = [jnp.zeros((8, WIDTH), F32)]
    near = [jnp.where(odd, low, high) for low, high in planes]
    far = [jnp.where(odd, high, low) for low, high in planes]
    near_ref[...] = jnp.concatenate(near + pad, 0).astype(near_ref.dtype)
    far_ref[...] = jnp.concatenate(far + pad, 0).astype(far_ref.dtype)


def box(number):
    return pl.multiple_of((1 + number % 2) * ROWS, ROWS)


def first_kernel(odd_ref, start_ref, x_ref, y_ref, z_ref, h_ref, s_ref, near_ref, far_ref, v_ref):
    s_ref[ROWS:, :] = jnp.zeros((2 * ROWS, WIDTH), F32)
    for x in range(SIDE):
        for y in range(SIDE):
            if x < 6 and y < 6:
                line = start_ref[x, y]
            elif y < 6:
                line = x_ref[0, y]
            else:
                line = y_ref[x, 0]
            s_ref[pl.ds(ROWS + x * 8 + y, LAYERS - 1, stride=PLANE), :] = line.astype(F32)
        top = ROWS + (LAYERS - 1) * PLANE + x * 8
        s_ref[top : top + SIDE, :] = z_ref[x].astype(F32)
    for begin, size in CHUNKS:
        v_ref[begin : begin + size, :] = s_ref[ROWS + begin : ROWS + begin + size, :].astype(BF16)
    multiply(odd_ref, h_ref, s_ref, near_ref, far_ref, v_ref)


CHUNKS = [(i * 112, 112) for i in range(12)] + [(1344, 64)]


def recur(scale, shift, s_ref, below_ref, above_ref, now, old, begin, size):
    w = s_ref[begin : begin + size, :]
    for at, face_ref in ((0, below_ref), (CHUNKS[-1][0], above_ref)):
        if begin == at:
            rest = jnp.zeros((size - PLANE, WIDTH), F32)
            w = w + jnp.concatenate([face_ref[...].astype(F32), rest], 0)
    out = scale * (w - CENTER * s_ref[pl.ds(now + begin, size), :])
    return out - shift * s_ref[pl.ds(old + begin, size), :]


def step_kernel(
    odd_ref, index_ref, factor_ref, s_in, below, above, h_ref, s_ref, near_ref, far_ref, v_ref
):
    number = index_ref[0]
    scale, shift = factor_ref[2 * number], factor_ref[2 * number + 1]
    now, old = box(number), box(number + 1)
    for begin, size in CHUNKS:
        out = recur(scale, shift, s_in, below, above, now, old, begin, size)
        s_ref[pl.ds(old + begin, size), :] = out
        v_ref[begin : begin + size, :] = out.astype(BF16)
    multiply(odd_ref, h_ref, s_ref, near_ref, far_ref, v_ref)


def fold_x_kernel(odd_ref, w_in, near_ref, far_ref, w_ref, low_ref, high_ref):
    odd = odd_ref[0] == 1
    for z in range(LAYERS):
        near = near_ref[z * 8 : z * 8 + 8, :].astype(F32)
        far = far_ref[z * 8 : z * 8 + 8, :].astype(F32)
        for x, add in ((0, jnp.where(odd, near, far)), (ORDER, jnp.where(odd, far, near))):
            rows = slice(z * PLANE + x * 8, z * PLANE + x * 8 + 8)
            w_ref[rows, :] += add
    lines = LAYERS * SIDE
    for ref, y in ((low_ref, 0), (high_ref, ORDER)):
        face = w_ref[pl.ds(y, lines, stride=8), :]
        ref[...] = jnp.concatenate([face, jnp.zeros((1, WIDTH), F32)], 0).astype(ref.dtype)


def fold_y_kernel(w_in, below_ref, above_ref, w_ref, low_ref, high_ref):
    lines = LAYERS * SIDE
    for ref, y in ((below_ref, 0), (above_ref, ORDER)):
        rows = pl.ds(y, lines, stride=8)
        w_ref[rows, :] = w_ref[rows, :] + ref[...].astype(F32)[:lines]
    low_ref[...] = w_ref[:PLANE, :].astype(low_ref.dtype)
    high_ref[...] = w_ref[(LAYERS - 1) * PLANE : LAYERS * PLANE, :].astype(high_ref.dtype)


def last_kernel(scale, shift, s_ref, below, above, locked_ref, filtered_ref, parts_ref, field):
    now, old = (ROWS * (1 + (number % 2)) for number in (APPLY - 1, APPLY))
    for begin, size in CHUNKS:
        field[begin : begin + size, :] = recur(
            scale, shift, s_ref, below, above, now, old, begin, size
        )
    depth = LAYERS - 1
    for x in range(ORDER):
        for y in range(ORDER):
            at = (x * ORDER + y) * depth
            line = field[pl.ds(x * 8 + y, depth, stride=PLANE), :]
            filtered_ref[at : at + depth, :] = line.astype(BF16)
    f = filtered_ref[...]
    parts_ref[:128, :128] = lax.dot_general(f, f, CONTRACT, preferred_element_type=F32)
    for i, (r, c) in enumerate(((128, 0), (0, 128), (128, 128))):
        parts_ref[r : r + 128, c : c + 128] = lax.dot_general(
            locked_ref[:, i * 128 : i * 128 + 128], f, CONTRACT, preferred_element_type=F32
        )


def mesh_total(rows):
    odd = lax.axis_index("gx") % 2 == 1
    count = lax.axis_size("gx")
    partner = [(i, i ^ 1) for i in range(count)]
    lower, upper = jnp.split(rows, 2)
    other = lax.ppermute(jnp.where(odd, lower, upper), "gx", partner)
    half = jnp.where(odd, upper, lower) + other
    axes = ("gy", "gz")
    pieces = half.reshape(lax.axis_size(axes), -1, rows.shape[1])
    mine = lax.all_to_all(pieces, axes, 0, 0).sum(0)
    total = mine
    for step in range(2, count, 2):
        total = total + passed_along(mine, "gx", step)
    half = lax.all_to_all(jnp.broadcast_to(total, pieces.shape), axes, 0, 0).reshape(half.shape)
    other = lax.ppermute(half, "gx", partner)
    return jnp.concatenate([jnp.where(odd, other, half), jnp.where(odd, half, other)], 0)


PANEL = 16
PIVOTS = 8


def inverse_kernel(a_ref, out_ref, m_ref):
    size = a_ref.shape[0]
    m_ref[:, :size] = a_ref[...]
    r = lax.broadcasted_iota(jnp.int32, (size, size), 0)
    c = lax.broadcasted_iota(jnp.int32, (size, size), 1)
    m_ref[:, size:] = jnp.where(r == c, 1.0, 0.0)
    line = lax.broadcasted_iota(jnp.int32, (PANEL, 2 * size), 0)

    def panel(step, carry):
        p = m_ref[:PANEL, :]
        scale = jnp.ones((PANEL, 2 * size), F32)
        for i in range(0, PANEL, PIVOTS):
            span = range(PIVOTS)
            rows = [jnp.broadcast_to(p[i + u : i + u + 1, :], p.shape) for u in span]
            cols = [jnp.broadcast_to(p[:, i + u : i + u + 1], p.shape) for u in span]
            s = [
                [jnp.broadcast_to(rows[u][:, i + v : i + v + 1], p.shape) for v in span]
                for u in span
            ]
            for u in span:
                inv = 1.0 / s[u][u]
                scale = jnp.where(line == i + u, lax.rsqrt(s[u][u]), scale)
                for v in range(u + 1, PIVOTS):
                    f = s[u][v] * inv
                    rows[v] = rows[v] - f * rows[u]
                    cols[v] = cols[v] - f * cols[u]
                    for w in range(v, PIVOTS):
                        s[v][w] = s[v][w] - f * s[u][w]
                cols[u] = cols[u] * inv
            new = p
            for u in span:
                new = new - cols[u] * rows[u]
            p = jnp.where(line >= i + PIVOTS, new, p)
            for u in span:
                p = jnp.where(line == i + u, rows[u], p)
        p = p * scale
        out_ref[pl.ds(pl.multiple_of(step * PANEL, PANEL), PANEL), :] = p[:, size:]
        update = lax.dot_general(
            p[:, :size], p, CONTRACT, precision=lax.Precision.HIGHEST, preferred_element_type=F32
        )
        left = m_ref[PANEL:, :] - update[PANEL:, :]
        m_ref[: size - PANEL, :size] = pltpu.roll(left[:, :size], size - PANEL, 1)
        m_ref[: size - PANEL, size:] = left[:, size:]
        return carry

    lax.fori_loop(0, size // PANEL, panel, 0)


def normalize(gram_matrix, vectors):
    size = gram_matrix.shape[0]
    inverse = call(
        inverse_kernel, [((size, size), F32)], 1, scratch=(pltpu.VMEM((size, 2 * size), F32),)
    )(gram_matrix)[0]
    return lax.dot_general(
        vectors,
        inverse,
        (((1,), (1,)), ((), ())),
        precision=lax.Precision.HIGHEST,
        preferred_element_type=F32,
    )


LINK = BF16


def per_device(start_block, locked_orbitals, cell_h):
    devices = lax.axis_size(AXES)
    nodes_total = float(
        start_block.shape[0] * start_block.shape[1] * start_block.shape[2] * devices
    )
    rim_x = passed_along(start_block[0:1], "gx", -1)
    low_y = jnp.concatenate([start_block[:, 0:1], rim_x[:, 0:1]], 0)
    rim_y = passed_along(low_y, "gy", -1)
    low_z = jnp.concatenate([start_block[:, :, 0], rim_x[:, :, 0]], 0)
    low_z = jnp.concatenate([low_z, rim_y[:, :, 0]], 1)
    rim_z = passed_along(low_z, "gz", -1)
    h = call(order_kernel, [((CELLS, CELL_OUT, CELL_IN), BF16)], 1, cost=4_000_000)(
        cell_h.reshape(CELLS, NODE, NODE)
    )[0]
    h = pltpu.with_memory_space_constraint(h, pltpu.VMEM)
    locked_flat = locked_orbitals.reshape(-1, LOCKED)
    wide = [locked_flat[:, i : i + 128] for i in range(0, LOCKED, 128)]
    blocks = [
        lax.dot_general(wide[j], wide[i], CONTRACT, preferred_element_type=F32)
        for i in range(3)
        for j in range(i, 3)
    ]
    locked_parts = jnp.concatenate(
        [jnp.concatenate(blocks[i : i + 2], 0) for i in (0, 2, 4)], 1
    )

    state = ((3 * ROWS, WIDTH), F32)
    fields = [state, ((208, WIDTH), LINK), ((208, WIDTH), LINK)]
    scratch = (pltpu.VMEM((ROWS, WIDTH), BF16),)
    odd = (lax.axis_index("gx") % 2).astype(jnp.int32).reshape(1)
    carry = call(first_kernel, fields, 5, scratch=scratch, scalars=1)(
        odd, start_block, rim_x, rim_y, rim_z, h
    )
    factors, sigma = [(SIGMA / HALF, 0.0)], SIGMA
    for repeat in range(APPLY - 1):
        following = 1.0 / (2.0 / SIGMA - sigma)
        factors.append((2.0 * following / HALF, sigma * following))
        sigma = following
    table = jnp.array(factors[:-1], F32).reshape(-1)

    def exchange(s, near, far):
        near, far = swapped(near, far)
        s, low, high = call(
            fold_x_kernel, [state] + [((176, WIDTH), LINK)] * 2, 3, aliases={1: 0}, scalars=1
        )(odd, s, near, far)
        below, above = both_ways(low, high, "gy")
        s, low, high = call(
            fold_y_kernel, [state] + [((PLANE, WIDTH), LINK)] * 2, 3, aliases={0: 0}
        )(s, below, above)
        below, above = both_ways(low, high, "gz")
        return s, below, above

    def apply(number, carry):
        index = jnp.asarray(number, jnp.int32).reshape(1)
        s, near, far = call(
            step_kernel, fields, 4, scratch=scratch, scalars=3, aliases={3: 0}
        )(odd, index, table, *exchange(*carry), h)
        return pltpu.with_memory_space_constraint(s, pltpu.VMEM), near, far

    carry = lax.fori_loop(1, APPLY - 1, apply, apply(0, carry))
    scale, shift = factors[-1]
    filtered, parts = call(
        functools.partial(last_kernel, scale, shift),
        [((864, WIDTH), BF16), ((256, 256), F32)],
        4,
        scratch=(pltpu.VMEM((ROWS, WIDTH), F32),),
    )(*exchange(*carry), locked_flat)
    total = mesh_total(jnp.concatenate([parts, locked_parts], 1))
    g = [total[r : r + 128, c : c + 128] for c in (256, 384, 512) for r in (0, 128)]
    locked_gram = jnp.concatenate(
        [
            jnp.concatenate([g[0], g[1].T, g[2].T], 1),
            jnp.concatenate([g[1], g[3], g[4].T], 1),
            jnp.concatenate([g[2], g[4], g[5]], 1),
        ],
        0,
    )
    self_gram = total[:128, :128]
    cross = jnp.concatenate([total[128:, :128], total[:128, 128:256], total[128:, 128:256]], 0)
    coefficient = (cross / nodes_total).astype(BF16)
    coef_wide = coefficient.astype(F32)
    projected = filtered.astype(F32) - jnp.dot(
        locked_flat, coefficient, preferred_element_type=F32
    )
    precise = dict(precision=lax.Precision.HIGHEST, preferred_element_type=F32)
    mixed = lax.dot_general(cross, coef_wide, CONTRACT, **precise)
    weighted = jnp.dot(locked_gram, coef_wide, **precise)
    quadratic = lax.dot_general(coef_wide, weighted, CONTRACT, **precise)
    gram_matrix = (self_gram - mixed - mixed.T + quadratic) / nodes_total
    result = normalize(gram_matrix, projected)
    return result.reshape(start_block.shape)


def solution(mesh):
    placed = (P("gx", "gy", "gz", None), P("gx", "gy", "gz", None), P("gx", "gy", "gz", None, None))
    return jax.shard_map(
        per_device, mesh=mesh, in_specs=placed, out_specs=P("gx", "gy", "gz", None), check_vma=False
    )
```

```python
import functools

import jax
import jax.numpy as jnp
from jax import lax
from jax.experimental import pallas as pl
from jax.experimental.pallas import tpu as pltpu
from jax.sharding import PartitionSpec as P


ORDER = 6
SIDE = 7
NODE = 343
APPLY = 6
LOCKED = 384
WIDTH = 128

PLANE = 56
CELLS = 4
LAYERS = 6 * CELLS + 1
ROWS = 1408
STEP = 6 * PLANE
CELL_OUT = SIDE * PLANE
CELL_IN = CELL_OUT + 8

filter_low = 3.0
filter_high = 40.0
filter_bottom = 0.5
HALF = (filter_high - filter_low) / 2.0
CENTER = (filter_high + filter_low) / 2.0
SIGMA = HALF / (filter_bottom - CENTER)

F32 = jnp.float32
BF16 = jnp.bfloat16
AXES = ("gx", "gy", "gz")
CONTRACT = (((0,), (0,)), ((), ()))
PARAMS = pltpu.CompilerParams(vmem_limit_bytes=16 * 2**20)
VM = pl.BlockSpec(memory_space=pltpu.VMEM)
SM = pl.BlockSpec(memory_space=pltpu.SMEM)


def call(kernel, outs, n_in, cost=1_000_000, scratch=(), aliases=None, scalars=0):
    return pl.pallas_call(
        kernel,
        out_shape=[jax.ShapeDtypeStruct(s, d) for s, d in outs],
        in_specs=[SM] * scalars + [VM] * n_in,
        out_specs=[VM] * len(outs),
        scratch_shapes=list(scratch),
        input_output_aliases=aliases or {},
        compiler_params=PARAMS,
        cost_estimate=pl.CostEstimate(flops=cost, bytes_accessed=cost, transcendentals=0),
    )


def passed_along(block, axis, distance):
    devices = range(lax.axis_size(axis))
    route = [((i - distance) % len(devices), i) for i in devices]
    return lax.ppermute(block, axis, route)


def swapped(near, far):
    count = lax.axis_size("gx")
    partner = [(i, i ^ 1) for i in range(count)]
    across = [(i, (i + 2 * (i % 2) - 1) % count) for i in range(count)]
    return lax.ppermute(near, "gx", partner), lax.ppermute(far, "gx", across)


def both_ways(low_face, high_face, axis):
    return passed_along(high_face, axis, 1), passed_along(low_face, axis, -1)


def order_kernel(h_ref, out_ref):
    row = lax.broadcasted_iota(jnp.int32, (CELL_IN, NODE), 0)
    col = lax.broadcasted_iota(jnp.int32, (CELL_IN, NODE), 1)
    z, rest = row // PLANE, row % PLANE
    x, y = rest // 8, rest % 8
    pick = jnp.where((x * 49 + y * 7 + z == col) & (y < SIDE) & (z < SIDE), 1.0, 0.0).astype(BF16)
    for k in range(CELLS):
        half = jnp.dot(pick[:CELL_OUT], h_ref[k], preferred_element_type=F32).astype(BF16)
        out_ref[k] = lax.dot_general(
            half, pick, (((1,), (1,)), ((), ())), preferred_element_type=F32
        ).astype(BF16)


def multiply(odd_ref, h_ref, w_ref, near_ref, far_ref, v_ref):
    planes, top = [], None
    for k in range(CELLS):
        y = jnp.dot(h_ref[k], v_ref[k * STEP : k * STEP + CELL_IN, :], preferred_element_type=F32)
        pieces = [y[j * PLANE : (j + 1) * PLANE] for j in range(SIDE)]
        if top is not None:
            pieces[0] = pieces[0] + top
        top = pieces.pop()
        if k == CELLS - 1:
            pieces.append(top)
        for piece in pieces:
            at = len(planes) * PLANE
            w_ref[at : at + PLANE, :] = piece
            planes.append((piece[:8], piece[ORDER * 8 :]))
    w_ref[LAYERS * PLANE : ROWS, :] = jnp.zeros((ROWS - LAYERS * PLANE, WIDTH), F32)
    odd = odd_ref[0] == 1
    pad = [jnp.zeros((8, WIDTH), F32)]
    near = [jnp.where(odd, low, high) for low, high in planes]
    far = [jnp.where(odd, high, low) for low, high in planes]
    near_ref[...] = jnp.concatenate(near + pad, 0).astype(near_ref.dtype)
    far_ref[...] = jnp.concatenate(far + pad, 0).astype(far_ref.dtype)


def box(number):
    return pl.multiple_of((1 + number % 2) * ROWS, ROWS)


def first_kernel(odd_ref, start_ref, x_ref, y_ref, z_ref, h_ref, s_ref, near_ref, far_ref, v_ref):
    s_ref[ROWS:, :] = jnp.zeros((2 * ROWS, WIDTH), F32)
    for x in range(SIDE):
        for y in range(SIDE):
            if x < 6 and y < 6:
                line = start_ref[x, y]
            elif y < 6:
                line = x_ref[0, y]
            else:
                line = y_ref[x, 0]
            s_ref[pl.ds(ROWS + x * 8 + y, LAYERS - 1, stride=PLANE), :] = line.astype(F32)
        top = ROWS + (LAYERS - 1) * PLANE + x * 8
        s_ref[top : top + SIDE, :] = z_ref[x].astype(F32)
    for begin, size in CHUNKS:
        v_ref[begin : begin + size, :] = s_ref[ROWS + begin : ROWS + begin + size, :].astype(BF16)
    multiply(odd_ref, h_ref, s_ref, near_ref, far_ref, v_ref)


CHUNKS = [(i * 112, 112) for i in range(12)] + [(1344, 64)]


def recur(scale, shift, s_ref, below_ref, above_ref, now, old, begin, size):
    w = s_ref[begin : begin + size, :]
    for at, face_ref in ((0, below_ref), (CHUNKS[-1][0], above_ref)):
        if begin == at:
            rest = jnp.zeros((size - PLANE, WIDTH), F32)
            w = w + jnp.concatenate([face_ref[...].astype(F32), rest], 0)
    out = scale * (w - CENTER * s_ref[pl.ds(pl.multiple_of(now + begin, 16), size), :])
    return out - shift * s_ref[pl.ds(pl.multiple_of(old + begin, 16), size), :]


def step_kernel(
    odd_ref, index_ref, factor_ref, s_in, below, above, h_ref, s_ref, near_ref, far_ref, v_ref
):
    number = index_ref[0]
    scale, shift = factor_ref[2 * number], factor_ref[2 * number + 1]
    now, old = box(number), box(number + 1)
    for begin, size in CHUNKS:
        out = recur(scale, shift, s_in, below, above, now, old, begin, size)
        s_ref[pl.ds(pl.multiple_of(old + begin, 16), size), :] = out
        v_ref[begin : begin + size, :] = out.astype(BF16)
    multiply(odd_ref, h_ref, s_ref, near_ref, far_ref, v_ref)


def fold_x_kernel(odd_ref, w_in, near_ref, far_ref, w_ref, low_ref, high_ref):
    odd = odd_ref[0] == 1
    for z in range(LAYERS):
        near = near_ref[z * 8 : z * 8 + 8, :].astype(F32)
        far = far_ref[z * 8 : z * 8 + 8, :].astype(F32)
        for x, add in ((0, jnp.where(odd, near, far)), (ORDER, jnp.where(odd, far, near))):
            rows = slice(z * PLANE + x * 8, z * PLANE + x * 8 + 8)
            w_ref[rows, :] += add
    lines = LAYERS * SIDE
    for ref, y in ((low_ref, 0), (high_ref, ORDER)):
        face = w_ref[pl.ds(y, lines, stride=8), :]
        ref[...] = jnp.concatenate([face, jnp.zeros((1, WIDTH), F32)], 0).astype(ref.dtype)


def fold_y_kernel(w_in, below_ref, above_ref, w_ref, low_ref, high_ref):
    lines = LAYERS * SIDE
    for ref, y in ((below_ref, 0), (above_ref, ORDER)):
        rows = pl.ds(y, lines, stride=8)
        w_ref[rows, :] = w_ref[rows, :] + ref[...].astype(F32)[:lines]
    low_ref[...] = w_ref[:PLANE, :].astype(low_ref.dtype)
    high_ref[...] = w_ref[(LAYERS - 1) * PLANE : LAYERS * PLANE, :].astype(high_ref.dtype)


def last_kernel(scale, shift, s_ref, below, above, locked_ref, filtered_ref, parts_ref, field):
    now, old = (ROWS * (1 + (number % 2)) for number in (APPLY - 1, APPLY))
    for begin, size in CHUNKS:
        field[begin : begin + size, :] = recur(
            scale, shift, s_ref, below, above, now, old, begin, size
        )
    depth = LAYERS - 1
    for x in range(ORDER):
        for y in range(ORDER):
            at = (x * ORDER + y) * depth
            line = field[pl.ds(x * 8 + y, depth, stride=PLANE), :]
            filtered_ref[at : at + depth, :] = line.astype(BF16)
    f = filtered_ref[...]
    parts_ref[:128, :128] = lax.dot_general(f, f, CONTRACT, preferred_element_type=F32)
    for i, (r, c) in enumerate(((128, 0), (0, 128), (128, 128))):
        parts_ref[r : r + 128, c : c + 128] = lax.dot_general(
            locked_ref[:, i * 128 : i * 128 + 128], f, CONTRACT, preferred_element_type=F32
        )


def mesh_total(rows):
    odd = lax.axis_index("gx") % 2 == 1
    count = lax.axis_size("gx")
    partner = [(i, i ^ 1) for i in range(count)]
    lower, upper = jnp.split(rows, 2)
    other = lax.ppermute(jnp.where(odd, lower, upper), "gx", partner)
    half = jnp.where(odd, upper, lower) + other
    axes = ("gy", "gz")
    pieces = half.reshape(lax.axis_size(axes), -1, rows.shape[1])
    mine = lax.all_to_all(pieces, axes, 0, 0).sum(0)
    total = mine
    for step in range(2, count, 2):
        total = total + passed_along(mine, "gx", step)
    half = lax.all_to_all(jnp.broadcast_to(total, pieces.shape), axes, 0, 0).reshape(half.shape)
    other = lax.ppermute(half, "gx", partner)
    return jnp.concatenate([jnp.where(odd, other, half), jnp.where(odd, half, other)], 0)


PANEL = 16
PIVOTS = 8


def inverse_kernel(a_ref, out_ref, m_ref):
    size = a_ref.shape[0]
    m_ref[:, :size] = a_ref[...]
    r = lax.broadcasted_iota(jnp.int32, (size, size), 0)
    c = lax.broadcasted_iota(jnp.int32, (size, size), 1)
    m_ref[:, size:] = jnp.where(r == c, 1.0, 0.0)
    line = lax.broadcasted_iota(jnp.int32, (PANEL, 2 * size), 0)

    def panel(step, carry):
        p = m_ref[:PANEL, :]
        scale = jnp.ones((PANEL, 2 * size), F32)
        for i in range(0, PANEL, PIVOTS):
            span = range(PIVOTS)
            rows = [jnp.broadcast_to(p[i + u : i + u + 1, :], p.shape) for u in span]
            cols = [jnp.broadcast_to(p[:, i + u : i + u + 1], p.shape) for u in span]
            s = [
                [jnp.broadcast_to(rows[u][:, i + v : i + v + 1], p.shape) for v in span]
                for u in span
            ]
            for u in span:
                inv = 1.0 / s[u][u]
                scale = jnp.where(line == i + u, lax.rsqrt(s[u][u]), scale)
                for v in range(u + 1, PIVOTS):
                    f = s[u][v] * inv
                    rows[v] = rows[v] - f * rows[u]
                    cols[v] = cols[v] - f * cols[u]
                    for w in range(v, PIVOTS):
                        s[v][w] = s[v][w] - f * s[u][w]
                cols[u] = cols[u] * inv
            new = p
            for u in span:
                new = new - cols[u] * rows[u]
            p = jnp.where(line >= i + PIVOTS, new, p)
            for u in span:
                p = jnp.where(line == i + u, rows[u], p)
        p = p * scale
        out_ref[pl.ds(pl.multiple_of(step * PANEL, PANEL), PANEL), :] = p[:, size:]
        update = lax.dot_general(
            p[:, :size], p, CONTRACT, precision=lax.Precision.HIGHEST, preferred_element_type=F32
        )
        left = m_ref[PANEL:, :] - update[PANEL:, :]
        m_ref[: size - PANEL, :size] = pltpu.roll(left[:, :size], size - PANEL, 1)
        m_ref[: size - PANEL, size:] = left[:, size:]
        return carry

    lax.fori_loop(0, size // PANEL, panel, 0)


def normalize(gram_matrix, vectors):
    size = gram_matrix.shape[0]
    inverse = call(
        inverse_kernel, [((size, size), F32)], 1, scratch=(pltpu.VMEM((size, 2 * size), F32),)
    )(gram_matrix)[0]
    return lax.dot_general(
        vectors,
        inverse,
        (((1,), (1,)), ((), ())),
        precision=lax.Precision.HIGHEST,
        preferred_element_type=F32,
    )


LINK = BF16


def per_device(start_block, locked_orbitals, cell_h):
    devices = lax.axis_size(AXES)
    nodes_total = float(
        start_block.shape[0] * start_block.shape[1] * start_block.shape[2] * devices
    )
    rim_x = passed_along(start_block[0:1], "gx", -1)
    low_y = jnp.concatenate([start_block[:, 0:1], rim_x[:, 0:1]], 0)
    rim_y = passed_along(low_y, "gy", -1)
    low_z = jnp.concatenate([start_block[:, :, 0], rim_x[:, :, 0]], 0)
    low_z = jnp.concatenate([low_z, rim_y[:, :, 0]], 1)
    rim_z = passed_along(low_z, "gz", -1)
    h = call(order_kernel, [((CELLS, CELL_OUT, CELL_IN), BF16)], 1, cost=4_000_000)(
        cell_h.reshape(CELLS, NODE, NODE)
    )[0]
    h = pltpu.with_memory_space_constraint(h, pltpu.VMEM)
    locked_flat = locked_orbitals.reshape(-1, LOCKED)
    wide = [locked_flat[:, i : i + 128] for i in range(0, LOCKED, 128)]
    blocks = [
        lax.dot_general(wide[j], wide[i], CONTRACT, preferred_element_type=F32)
        for i in range(3)
        for j in range(i, 3)
    ]
    locked_parts = jnp.concatenate(
        [jnp.concatenate(blocks[i : i + 2], 0) for i in (0, 2, 4)], 1
    )

    state = ((3 * ROWS, WIDTH), F32)
    fields = [state, ((208, WIDTH), LINK), ((208, WIDTH), LINK)]
    scratch = (pltpu.VMEM((ROWS, WIDTH), BF16),)
    odd = (lax.axis_index("gx") % 2).astype(jnp.int32).reshape(1)
    carry = call(first_kernel, fields, 5, scratch=scratch, scalars=1)(
        odd, start_block, rim_x, rim_y, rim_z, h
    )
    factors, sigma = [(SIGMA / HALF, 0.0)], SIGMA
    for repeat in range(APPLY - 1):
        following = 1.0 / (2.0 / SIGMA - sigma)
        factors.append((2.0 * following / HALF, sigma * following))
        sigma = following
    table = jnp.array(factors[:-1], F32).reshape(-1)

    def exchange(s, near, far):
        near, far = swapped(near, far)
        s, low, high = call(
            fold_x_kernel, [state] + [((176, WIDTH), LINK)] * 2, 3, aliases={1: 0}, scalars=1
        )(odd, s, near, far)
        below, above = both_ways(low, high, "gy")
        s, low, high = call(
            fold_y_kernel, [state] + [((PLANE, WIDTH), LINK)] * 2, 3, aliases={0: 0}
        )(s, below, above)
        below, above = both_ways(low, high, "gz")
        return s, below, above

    def apply(number, carry):
        index = jnp.asarray(number, jnp.int32).reshape(1)
        s, near, far = call(
            step_kernel, fields, 4, scratch=scratch, scalars=3, aliases={3: 0}
        )(odd, index, table, *exchange(*carry), h)
        return pltpu.with_memory_space_constraint(s, pltpu.VMEM), near, far

    carry = lax.fori_loop(1, APPLY - 1, apply, apply(0, carry))
    scale, shift = factors[-1]
    filtered, parts = call(
        functools.partial(last_kernel, scale, shift),
        [((864, WIDTH), BF16), ((256, 256), F32)],
        4,
        scratch=(pltpu.VMEM((ROWS, WIDTH), F32),),
    )(*exchange(*carry), locked_flat)
    total = mesh_total(jnp.concatenate([parts, locked_parts], 1))
    g = [total[r : r + 128, c : c + 128] for c in (256, 384, 512) for r in (0, 128)]
    locked_gram = jnp.concatenate(
        [
            jnp.concatenate([g[0], g[1].T, g[2].T], 1),
            jnp.concatenate([g[1], g[3], g[4].T], 1),
            jnp.concatenate([g[2], g[4], g[5]], 1),
        ],
        0,
    )
    self_gram = total[:128, :128]
    cross = jnp.concatenate([total[128:, :128], total[:128, 128:256], total[128:, 128:256]], 0)
    coefficient = (cross / nodes_total).astype(BF16)
    coef_wide = coefficient.astype(F32)
    projected = filtered.astype(F32) - jnp.dot(
        locked_flat, coefficient, preferred_element_type=F32
    )
    precise = dict(precision=lax.Precision.HIGHEST, preferred_element_type=F32)
    mixed = lax.dot_general(cross, coef_wide, CONTRACT, **precise)
    weighted = jnp.dot(locked_gram, coef_wide, **precise)
    quadratic = lax.dot_general(coef_wide, weighted, CONTRACT, **precise)
    gram_matrix = (self_gram - mixed - mixed.T + quadratic) / nodes_total
    result = normalize(gram_matrix, projected)
    return result.reshape(start_block.shape)


def solution(mesh):
    placed = (P("gx", "gy", "gz", None), P("gx", "gy", "gz", None), P("gx", "gy", "gz", None, None))
    return jax.shard_map(
        per_device, mesh=mesh, in_specs=placed, out_specs=P("gx", "gy", "gz", None), check_vma=False
    )
```
